32 devices in a mesh: slab: 16 (over z, x, core), col: 2 (over y).
Axes of the slice: x: 2, y: 2, z: 4, core: 2. Of those that a mesh axis runs over, the one named last changes fastest.
Arguments:
- pressure: float32 [1024, 512], P('slab', 'col'), may hold values from 1 to 4
- storage: float32 [1024, 512], P('slab', 'col'), may hold values from 0.5 to 2
- trans: float32 [1024, 512], P('slab', 'col'), may hold values from 0.5 to 8
- source: float32 [1024, 512], P('slab', 'col'), may hold values from -1.2 to 1.2
- shells_old: float32 [2, 1024, 64, 128], P('col', 'slab'), may hold values from 1 to 2
- shell_cap: float32 [64], replicated, may hold values from 0.5 to 4
- shell_trans: float32 [64], replicated, may hold values from 0.5 to 4
- new_source: int32 [2, 512], P('col'), may hold values from 0 to 1023, as said below
- cell_block: int32 [2, 1024], P('col', 'slab'), may hold values from 0 to 127, as said below
Outputs:
- pressure_out: float32 [1024, 512], P('slab', 'col')
- shells_new: float32 [2, 512, 64, 128], P('col', 'slab')
The draws below stay inside these ranges and needn't reach their ends.
Inputs may be any that keep to these rules, and one draw needn't show every extreme that they name: `new_source`: within each col index, every old slot is taken at most once; the slots after the move on one slab device take blocks from 8 distinct slab devices, exactly 4 blocks from each; the taken old slots lie only on the even-numbered slab devices, each of which has all 64 of its slots taken. `cell_block`: within one slab device and col index the entries are distinct.
All inputs are finite; a program needn't handle non-finite values.
Results may differ from the reference program's by a relative error of at most 0.0003.
Values sent between devices are 32-bit elements; how exact they have to be, the bound alone decides.
No kernel may reach another device: no remote copies, remote signals or barrier semaphores. Data moves between devices by JAX's collectives and lax.ppermute only.
A program may use at most 128 MiB of HBM per device.

```python
import math
import jax
import jax.numpy as jnp
from jax import lax

CS = 64
CW = 256
CB = 128
SH = 64
CAP = 4
B_NEW = 32
STEPS = 2
ITERS = 3
B_OLD = 64
FB = 128
NX = 1024
NY = 512
NOLD = 1024
N_SLAB = 16
N_COL = 2


def draw_new_source(key, part):

    def one_col(col_key):
        key_order, key_old, key_new = jax.random.split(col_key, 3)
        order = jax.random.permutation(key_order, N_SLAB)
        shuffle_old = jax.random.permutation(key_old, B_OLD)
        shuffle_new = jax.random.permutation(key_new, B_NEW)
        half = N_SLAB // 2
        groups = B_NEW // CAP
        position = jnp.arange(N_SLAB)
        group_index = jnp.arange(groups)
        within = jnp.arange(CAP)
        source_dev = 2 * ((position[:, None] // 2 + group_index[None, :]) % half)
        group_old = 2 * group_index[None, :] + position[:, None] % 2
        local = shuffle_old[group_old[:, :, None] * CAP + within[None, None, :]]
        global_slot = source_dev[:, :, None] * B_OLD + local
        by_position = global_slot.reshape(N_SLAB, B_NEW)[:, shuffle_new]
        placed = jnp.zeros((N_SLAB, B_NEW), jnp.int32).at[order].set(by_position.astype(jnp.int32))
        return placed.reshape(-1)
    keys = jax.random.split(jax.random.fold_in(key, 11), N_COL)
    return jax.vmap(one_col)(keys).astype(jnp.int32)


def draw_cell_block(key, part):
    keys = jax.random.split(jax.random.fold_in(key, 23), N_COL * N_SLAB)
    chosen = jax.vmap(lambda one_key: jax.random.permutation(one_key, FB)[:B_OLD])(keys)
    return chosen.reshape(N_COL, N_SLAB * B_OLD).astype(jnp.int32)


def level_of(own_key, dims, pieces, low, largest):
    level, own = 1.0, jax.random.fold_in(own_key, 6)
    for dim, blocks in pieces:
        steps = jnp.exp(jax.random.uniform(jax.random.fold_in(own, dim), (blocks,), jnp.float32, low / len(pieces), largest / len(pieces)))
        level = level * jnp.repeat(steps, dims[dim] // blocks).reshape([-1 if axis == dim else 1 for axis in range(len(dims))])
    return level


def normal_values(own_key, extent, spread, bound, pieces=(), held_as=jnp.bfloat16):
    result = jax.random.normal(own_key, extent, jnp.float32) * spread
    if len(pieces) > 0:
        result = level_of(own_key, extent, pieces, -0.22, 0.18) * result
    return jnp.clip(result, min=-bound, max=bound).astype(held_as)


def setup_inputs(seed: int = 0) -> dict:
    splits = jax.random.split(jax.random.key(seed), 10)
    pressure = jnp.clip(1.0 + 3.0 * jax.random.uniform(splits[0], (NX, NY), jnp.float32) ** level_of(splits[0], (NX, NY), ((0, 16), (1, 2)), -0.2, 0.2), 1.0, 4.0)
    storage = jnp.clip(jnp.exp(math.log(2.0) - 1.3862944 * jax.random.uniform(splits[1], (NX, NY), jnp.float32) ** level_of(splits[1], (NX, NY), ((0, 16), (1, 2)), -0.2, 0.2)), 0.5, 2.0)
    trans = jnp.clip(jnp.exp(math.log(8.0) - 2.7725887 * jax.random.uniform(splits[2], (NX, NY), jnp.float32) ** level_of(splits[2], (NX, NY), ((0, 16), (1, 2)), -0.2, 0.2)), 0.5, 8.0)
    source = normal_values(splits[3], (NX, NY), 0.25, 1.2, ((0, 16), (1, 2)), jnp.float32)
    shells_old = jnp.clip(1.0 + 1.0 * jax.random.uniform(splits[4], (N_COL, NOLD, SH, CB), jnp.float32) ** level_of(splits[4], (N_COL, NOLD, SH, CB), ((0, 2), (1, 16)), -0.2, 0.2), 1.0, 2.0)
    shell_cap = jnp.clip(jnp.exp(jax.random.uniform(splits[5], (SH,), jnp.float32, math.log(0.5), math.log(4.0))), 0.5, 4.0)
    shell_trans = jnp.clip(jnp.exp(jax.random.uniform(splits[6], (SH,), jnp.float32, math.log(0.5), math.log(4.0))), 0.5, 4.0)
    new_source = draw_new_source(jax.random.fold_in(splits[9], 71), 0)
    cell_block = draw_cell_block(jax.random.fold_in(splits[9], 71), 0)
    return dict(pressure=pressure, storage=storage, trans=trans, source=source, shells_old=shells_old, shell_cap=shell_cap, shell_trans=shell_trans, new_source=new_source, cell_block=cell_block)


def shell_inverse(shell_cap, shell_trans):
    inner = jnp.concatenate([shell_trans[1:], jnp.zeros((1,), jnp.float32)])
    matrix = jnp.diag(shell_cap + shell_trans + inner) - jnp.diag(inner[:-1], 1) - jnp.diag(inner[:-1], -1)
    inverse = jnp.linalg.solve(matrix, jnp.eye(matrix.shape[0], dtype=jnp.float32))
    return (inverse, inverse[:, 0] * shell_trans[0])

def newton_update(pressure, padded, tpad, prev, storage, source, exchange_term, active, coupling):
    height, breadth = pressure.shape
    center = tpad[1:-1, 1:-1]
    flux = jnp.zeros_like(pressure)
    conduct = jnp.zeros_like(pressure)
    for shift_row, shift_col in ((0, 1), (2, 1), (1, 0), (1, 2)):
        near_p = padded[shift_row:shift_row + height, shift_col:shift_col + breadth]
        near_t = tpad[shift_row:shift_row + height, shift_col:shift_col + breadth]
        face = 2.0 * center * near_t / (center + near_t)
        flux = flux + face * 0.5 * (near_p + pressure) * (near_p - pressure)
        conduct = conduct + face
    misfit = storage * (pressure - prev) - flux + exchange_term - source
    slope = storage + pressure * conduct + active * coupling
    return pressure - misfit / slope

def reference(pressure, storage, trans, source, shells_old, shell_cap, shell_trans, new_source, cell_block):
    inverse, couple = shell_inverse(shell_cap, shell_trans)
    coupling = shell_trans[0] * (1.0 - couple[0])
    ncols = new_source.shape[0]
    per_row = CW // 128
    home = new_source // B_OLD
    fblock = jax.vmap(lambda table, index: table[index])(cell_block, new_source)
    row_of = home * CS + fblock // per_row
    start = jnp.arange(ncols, dtype=jnp.int32)[:, None] * CW + fblock % per_row * 128
    flat = ((row_of * NY + start)[..., None] + jnp.arange(CB, dtype=jnp.int32)).astype(jnp.int32)
    flat_all = flat.reshape(-1)
    state = jax.vmap(lambda table, index: table[index])(shells_old, new_source)
    active = jnp.zeros((NX * NY,), jnp.float32).at[flat_all].set(1.0).reshape(NX, NY)
    tpad = jnp.pad(trans, 1)
    current = pressure
    for step in range(STEPS):
        prev = current
        for sweep in range(ITERS):
            block_p = current.reshape(-1)[flat]
            scaled = shell_cap[None, None, :, None] * state
            shells = jnp.einsum('kl,nblc->nbkc', inverse, scaled, precision=lax.Precision.HIGHEST)
            shells = shells + couple[None, None, :, None] * block_p[:, :, None, :]
            flow = shell_trans[0] * (block_p - shells[:, :, 0, :])
            exchange_term = jnp.zeros((NX * NY,), jnp.float32).at[flat_all].add(flow.reshape(-1)).reshape(NX, NY)
            current = newton_update(current, jnp.pad(current, 1), tpad, prev, storage, source, exchange_term, active, coupling)
        state = shells
    return (current, state)
```

```python
import functools

import jax
import jax.numpy as jnp
from jax import lax
from jax.experimental import pallas as pl
from jax.experimental.pallas import tpu as pltpu
from jax.sharding import PartitionSpec as P

CAP = 4
STEPS = 2
ITERS = 3
EDGE = 8
LANES = 128
FIELDS = 7
FILL = (1.0, 1.0, 0.0, 0.0, 0.0, 0.0, 0.0)


VMEM = pl.BlockSpec(memory_space=pltpu.VMEM)
SMEM = pl.BlockSpec(memory_space=pltpu.SMEM)
ANY = pl.BlockSpec(memory_space=pl.ANY)


def iota(shape, dim):
    return lax.broadcasted_iota(jnp.int32, shape, dim)


def split_by(value, size):
    if size & (size - 1) == 0:
        return value >> (size.bit_length() - 1), value & (size - 1)
    return value // size, value % size


def column_of(row, eye):
    return jnp.sum(jnp.where(eye, row, 0.0), axis=1, keepdims=True)


def row_of(column, count):
    eye = iota((count, count), 0) == iota((count, count), 1)
    return jnp.sum(jnp.where(eye, column, 0.0), axis=0, keepdims=True)


def placed(target, value, count):
    width = target.shape[1]
    hit = iota((count, width), 0) == target
    column = jnp.sum(jnp.where(hit, value.astype(jnp.float32), 0.0), axis=1, keepdims=True)
    return row_of(column, count).astype(jnp.int32)


def inverse_of(cap_row, trans_row):
    count = cap_row.shape[1]
    rows, cols = iota((count, count), 0), iota((count, count), 1)
    eye = rows == cols
    cap = column_of(cap_row, eye)
    trans = column_of(trans_row, eye)
    above = column_of(trans_row, cols == rows + 1)
    shape = (count, LANES)
    diag = jnp.broadcast_to(cap + trans + above, shape)
    low = jnp.broadcast_to(jnp.where(iota((count, 1), 0) == 0, 0.0, trans), shape)
    high = jnp.broadcast_to(above, shape)
    rhs = jnp.where(iota(shape, 0) == iota(shape, 1), 1.0, 0.0)
    step = 1
    while step < count:
        down = functools.partial(pltpu.roll, shift=step, axis=0)
        up = functools.partial(pltpu.roll, shift=count - step, axis=0)
        alpha = low / down(diag)
        gamma = high / up(diag)
        diag = diag - alpha * down(high) - gamma * up(low)
        rhs = rhs + alpha * down(rhs) + gamma * up(rhs)
        low, high = alpha * down(low), gamma * up(high)
        step *= 2
    return rhs / diag, cap, trans


def pack_sides(get, rows):
    lane = iota((rows, LANES), 1)
    out = jnp.zeros((rows, LANES), jnp.float32)
    for f in range(FIELDS):
        value = get(f)
        first, last = value[:, :LANES], value[:, -LANES:]
        at = 2 * EDGE * f
        moved = pltpu.roll(first, at, axis=1) if at else first
        out = jnp.where((lane >= at) & (lane < at + EDGE), moved, out)
        moved = pltpu.roll(last, (at + 2 * EDGE) % LANES, axis=1)
        out = jnp.where((lane >= at + EDGE) & (lane < at + 2 * EDGE), moved, out)
    return out


def base_kernel(
    cap_ref, trans_ref, table_ref, block_ref, shells_ref, p_ref, storage_ref, t_ref, source_ref,
    inv_ref, const_ref, slot_ref, recv_ref, precv_ref, b1_ref, b2_ref, e_ref, a_ref, b_ref, side_ref,
    held, tiles, sem,
):
    me = lax.axis_index("slab")
    slabs = lax.axis_size("slab")
    even = me % 2 == 0
    old_slots, count, _ = shells_ref.shape
    chunks = 4
    per = old_slots // chunks

    def chunk(i):
        part = pl.ds(i * per, per)
        return pltpu.make_async_copy(shells_ref.at[part], held.at[part], sem.at[i])

    @pl.when(even)
    def _():
        for i in range(chunks):
            chunk(i).start()

    cap_row, trans_row = cap_ref[...], trans_ref[...]
    inverse, cap, trans = inverse_of(cap_row, trans_row)
    inv_ref[...] = inverse
    t0 = trans_row[:, 0:1]
    first_row = inverse[0:1, :count] * cap_row
    w1 = inverse[:, 0:1] * cap
    w2 = cap * jnp.sum(inverse[:, :count] * first_row, axis=1, keepdims=True)
    couple_row = inverse[0:1, :count] * t0
    c0 = couple_row[:, 0:1]
    c1 = jnp.sum(first_row * couple_row, axis=1, keepdims=True)
    coupling = t0 * (1.0 - c0)
    const_ref[...] = jnp.broadcast_to(t0 * c1 / coupling, const_ref.shape)

    tiles[...] = jnp.zeros_like(tiles)

    @pl.when(even)
    def _():
        v1 = jnp.broadcast_to(t0 * w1, (count, LANES))
        v2 = jnp.broadcast_to(t0 * w2, (count, LANES))
        on = jnp.broadcast_to(coupling, (1, LANES))
        per_row = p_ref.shape[1] // LANES
        for i in range(chunks):
            chunk(i).wait()

            def body(j, carry):
                for u in range(4):
                    slot = i * per + j * 4 + u
                    data = held[slot]
                    row, half = split_by(block_ref[0, slot], per_row)
                    at = pl.ds(row, 1)
                    tiles[0, half, at] = jnp.sum(v1 * data, axis=0, keepdims=True)
                    tiles[1, half, at] = jnp.sum(v2 * data, axis=0, keepdims=True)
                    tiles[2, half, at] = on
                return carry

            lax.fori_loop(0, per // 4, body, 0)

    for i, ref in enumerate((b1_ref, b2_ref, e_ref)):
        ref[...] = jnp.concatenate([tiles[i, h] for h in range(tiles.shape[1])], axis=1)
    fields = (p_ref, storage_ref, t_ref, source_ref, b1_ref, b2_ref, e_ref)
    height = p_ref.shape[0]
    for f, ref in enumerate(fields):
        top, bottom = ref[0:EDGE, :], ref[height - EDGE : height, :]
        a_ref[f] = jnp.where(even, bottom, top)
        b_ref[f] = jnp.where(even, top, bottom)
    side_ref[...] = pack_sides(lambda f: fields[f][...], height)

    table = table_ref[...]
    total = table.shape[1]
    new_slots = total // slabs
    anchor, local = split_by(table, old_slots)
    lane = iota((1, total), 1)
    dest, within = split_by(lane, new_slots)
    rank = jnp.zeros((1, total), jnp.int32)
    for shift in range(1, new_slots):
        same = (pltpu.roll(anchor, shift, axis=1) == anchor) & (within >= shift)
        rank = rank + jnp.where(same, 1, 0)
    rank = jnp.minimum(rank, CAP - 1)
    mine = anchor == me - me % 2
    slot_ref[...] = placed(jnp.where(mine, dest * CAP + rank, -1), local, slabs * CAP)
    recv = ((anchor >> 1) ^ (me // 2)) * CAP + rank
    recv_ref[...] = placed(lane - me * new_slots, recv, new_slots)
    precv_ref[...] = placed(lane - me * new_slots, anchor * CAP + rank, new_slots)


def pack_kernel(slot_ref, own_ref, other_ref, *rest):
    *out_refs, held, in_sem, out_sem = rest
    me = lax.axis_index("slab")
    chip, core = me // 2, me % 2
    order = list(range(len(out_refs)))[::-1]

    def reads(source):
        for i, k in enumerate(order):
            for r in range(CAP):
                slot = slot_ref[0, ((chip ^ k) * 2 + core) * CAP + r]
                pltpu.make_async_copy(
                    source.at[slot], held.at[k * CAP + r], in_sem.at[k * CAP + r]
                ).start()

    @pl.when(core == 0)
    def _():
        reads(own_ref)

    @pl.when(core == 1)
    def _():
        reads(other_ref)

    def write(k):
        return pltpu.make_async_copy(
            held.at[pl.ds(k * CAP, CAP)], out_refs[k], out_sem.at[k]
        )

    for k in order:
        for r in range(CAP):
            pltpu.make_async_copy(
                own_ref.at[0], held.at[k * CAP + r], in_sem.at[k * CAP + r]
            ).wait()
        write(k).start()
    for k in order:
        write(k).wait()


def side_kernel(side_ref, a_ref, b_ref, out_ref):
    even = lax.axis_index("slab") % 2 == 0
    height = side_ref.shape[0]
    from_a = pack_sides(lambda f: a_ref[f], EDGE)
    from_b = pack_sides(lambda f: b_ref[f], EDGE)
    out_ref[0:EDGE] = jnp.where(even, from_b, from_a)
    out_ref[EDGE : EDGE + height] = side_ref[...]
    out_ref[EDGE + height :] = jnp.where(even, from_a, from_b)


def fracture_kernel(
    slot_ref, block_ref, const_ref, p_ref, storage_ref, t_ref, source_ref, b1_ref, b2_ref, e_ref,
    a_ref, b_ref, c_ref, d_ref, out_ref, rows_ref, keep,
):
    me, slabs = lax.axis_index("slab"), lax.axis_size("slab")
    col, cols = lax.axis_index("col"), lax.axis_size("col")
    even, col_even = me % 2 == 0, col % 2 == 0
    height, width = p_ref.shape
    tall, wide = height + 2 * EDGE, width + LANES
    row, lane = iota((tall, wide), 0), iota((tall, wide), 1)
    missing = (
        ((me == 0) & (row < EDGE))
        | ((me == slabs - 1) & (row >= EDGE + height))
        | ((lane >= width) & (lane < wide - EDGE) & ((lane >= width + EDGE) | (col == cols - 1)))
        | ((lane >= wide - EDGE) & (col == 0))
    )
    side_lane = iota((tall, LANES), 1)
    right = jnp.where(col_even, c_ref[...], d_ref[...])
    left = jnp.where(col_even, d_ref[...], c_ref[...])
    refs = (p_ref, storage_ref, t_ref, source_ref, b1_ref, b2_ref, e_ref)

    def extended(f):
        top = jnp.where(even, b_ref[f], a_ref[f])
        bottom = jnp.where(even, a_ref[f], b_ref[f])
        own = jnp.concatenate([top, refs[f][...], bottom], axis=0)
        at = 2 * EDGE * f
        from_right = pltpu.roll(right, LANES - at, axis=1) if at else right
        from_left = pltpu.roll(left, LANES - 2 * EDGE - at, axis=1)
        side = jnp.where(side_lane < EDGE, from_right, from_left)
        return jnp.where(missing, FILL[f], jnp.concatenate([own, side], axis=1))

    p, storage, t, source, base1, base2, coef = (extended(f) for f in range(FIELDS))
    next_lane = functools.partial(pltpu.roll, shift=wide - 1, axis=1)
    prev_lane = functools.partial(pltpu.roll, shift=1, axis=1)
    next_row = functools.partial(pltpu.roll, shift=tall - 1, axis=0)
    prev_row = functools.partial(pltpu.roll, shift=1, axis=0)

    def face_of(near):
        total = t + near
        return jnp.where(total > 0.0, 2.0 * t * near / jnp.where(total > 0.0, total, 1.0), 0.0)

    face_h, face_v = face_of(next_lane(t)), face_of(next_row(t))
    conduct = face_h + prev_lane(face_h) + face_v + prev_row(face_v)
    half_h, half_v = face_h * 0.5, face_v * 0.5
    fixed = storage + coef
    rhs = source + base1
    ratio = const_ref[0, 0]
    for step in range(STEPS):
        prev = p
        for sweep in range(ITERS):
            if sweep == ITERS - 1:
                mid = p[EDGE : EDGE + height]
                for h in range(width // LANES):
                    keep[step, h] = mid[:, h * LANES : (h + 1) * LANES]
                last = p
            near = next_lane(p)
            flow_h = half_h * (near + p) * (near - p)
            near = next_row(p)
            flow_v = half_v * (near + p) * (near - p)
            flux = flow_h - prev_lane(flow_h) + flow_v - prev_row(flow_v)
            misfit = storage * (p - prev) - flux + coef * p - rhs
            p = p - misfit / (fixed + p * conduct)
        rhs = source + base2 + ratio * coef * last
    out_ref[...] = p[EDGE : EDGE + height, :width]

    def body(d, carry):
        for r in range(CAP):
            fb = block_ref[0, slot_ref[0, d * CAP + r]]
            at_row, half = split_by(fb, width // LANES)
            for step in range(STEPS):
                rows_ref[d, pl.ds(step * CAP + r, 1)] = keep[step, half, pl.ds(at_row, 1)]
        return carry

    lax.fori_loop(0, slabs, body, 0)


def final_kernel(recv_ref, precv_ref, cap_ref, trans_ref, inv_ref, rows_ref, *rest):
    count_k = (len(rest) - 5)
    in_refs, (out_ref, held, done, in_sem, out_sem) = rest[:count_k], rest[count_k:]

    def read(k):
        return pltpu.make_async_copy(in_refs[k], held.at[pl.ds(k * CAP, CAP)], in_sem.at[k])

    for k in range(count_k):
        read(k).start()
    count = cap_ref.shape[1]
    cap_row = cap_ref[...]
    inverse = inv_ref[:, :count]
    t0 = trans_ref[:, 0:1]
    a = inverse * cap_row
    couple = inv_ref[:, 0:1] * t0
    couple2 = jnp.sum(a * (inverse[0:1, :] * t0), axis=1, keepdims=True)
    square = jnp.dot(a, a, preferred_element_type=jnp.float32, precision=lax.Precision.HIGHEST)
    high = square.astype(jnp.bfloat16)
    low = (square - high.astype(jnp.float32)).astype(jnp.bfloat16)
    left = jnp.concatenate([high, high, low], axis=1)
    m1 = jnp.broadcast_to(couple2, (count, LANES))
    m2 = jnp.broadcast_to(couple, (count, LANES))
    for k in range(count_k):
        read(k).wait()
    slots = out_ref.shape[0]
    pair = 2

    def write(j):
        part = pl.ds(j * pair, pair)
        return pltpu.make_async_copy(done.at[part], out_ref.at[part], out_sem.at[j])

    for j in range(slots // pair):
        parts = []
        for u in range(pair):
            data = held[recv_ref[0, j * pair + u]]
            hi = data.astype(jnp.bfloat16)
            lo = (data - hi.astype(jnp.float32)).astype(jnp.bfloat16)
            parts.append(jnp.concatenate([hi, lo, hi], axis=0))
        product = jnp.dot(left, jnp.concatenate(parts, axis=1), preferred_element_type=jnp.float32)
        for u in range(pair):
            where, r = split_by(precv_ref[0, j * pair + u], CAP)
            p1 = rows_ref[where, pl.ds(r, 1)]
            p2 = rows_ref[where, pl.ds(r + CAP, 1)]
            done[j * pair + u] = product[:, u * LANES : (u + 1) * LANES] + m1 * p1 + m2 * p2
        write(j).start()
    for j in range(slots // pair):
        write(j).wait()


def call(kernel, name, out_shape, in_specs, out_specs, args, scratch=(), cost=None):
    return pl.pallas_call(
        kernel,
        name=name,
        out_shape=out_shape,
        in_specs=in_specs,
        out_specs=out_specs,
        scratch_shapes=scratch,
        cost_estimate=cost,
    )(*args)


def f32(*shape):
    return jax.ShapeDtypeStruct(shape, jnp.float32)


def i32(*shape):
    return jax.ShapeDtypeStruct(shape, jnp.int32)


def swaps(size, odd):
    if not odd:
        return [(i, i ^ 1) for i in range(size)]
    return [(i, min(max(((i + 1) ^ 1) - 1, 0), size - 1)) for i in range(size)]


def shards(
    pressure, storage, trans, source, shells_old, shell_cap, shell_trans, new_source, cell_block
):
    slabs, cols = lax.axis_size("slab"), lax.axis_size("col")
    height, width = pressure.shape
    old_slots, count, cells = shells_old.shape[1:]
    new_slots = new_source.shape[1] // slabs
    chips = slabs // 2
    shells = shells_old[0]
    cap_row, trans_row = shell_cap.reshape(1, count), shell_trans.reshape(1, count)

    hopped = lax.ppermute(shells, "slab", swaps(slabs, False))
    (inverse, const, slot, recv, precv, base1, base2, coef, edge_a, edge_b, side) = call(
        base_kernel,
        "base",
        (
            f32(count, LANES), f32(1, LANES), i32(1, slabs * CAP), i32(1, new_slots), i32(1, new_slots),
            f32(height, width), f32(height, width), f32(height, width),
            f32(FIELDS, EDGE, width), f32(FIELDS, EDGE, width), f32(height, LANES),
        ),
        [VMEM, VMEM, VMEM, SMEM, ANY, VMEM, VMEM, VMEM, VMEM],
        (VMEM,) * 11,
        (cap_row, trans_row, new_source, cell_block, shells, pressure, storage, trans, source),
        [
            pltpu.VMEM((old_slots, count, cells), jnp.float32),
            pltpu.VMEM((3, width // LANES, height, LANES), jnp.float32),
            pltpu.SemaphoreType.DMA((4,)),
        ],
    )
    edge_b = lax.ppermute(edge_b, "slab", swaps(slabs, True))
    edge_a = lax.ppermute(edge_a, "slab", swaps(slabs, False))
    packed = call(
        pack_kernel,
        "pack",
        (f32(CAP, count, cells),) * chips,
        [SMEM, ANY, ANY],
        (ANY,) * chips,
        (slot, shells, hopped),
        [
            pltpu.VMEM((chips * CAP, count, cells), jnp.float32),
            pltpu.SemaphoreType.DMA((chips * CAP,)),
            pltpu.SemaphoreType.DMA((chips,)),
        ],
    )
    tall = height + 2 * EDGE
    side = call(
        side_kernel, "side", f32(tall, LANES), [VMEM] * 3, VMEM, (side, edge_a, edge_b)
    )
    side_c = lax.ppermute(side, "col", swaps(cols, False))
    side_d = lax.ppermute(side, "col", swaps(cols, True)) if cols > 2 else side_c

    arrived = [packed[0]]
    moved = {}
    for k in range(chips - 1, 0, -1):
        pairs = [(i, i ^ (2 * k)) for i in range(slabs)]
        moved[k] = lax.ppermute(packed[k], "slab", pairs)
    arrived += [moved[k] for k in range(1, chips)]

    result, rows = call(
        fracture_kernel,
        "fracture",
        (f32(height, width), f32(slabs, STEPS * CAP, LANES)),
        [SMEM, SMEM, SMEM] + [VMEM] * 11,
        (VMEM, VMEM),
        (
            slot, cell_block, const, pressure, storage, trans, source, base1, base2, coef,
            edge_a, edge_b, side_c, side_d,
        ),
        [pltpu.VMEM((STEPS, width // LANES, height, LANES), jnp.float32)],
    )
    rows = lax.all_to_all(rows, "slab", split_axis=0, concat_axis=0, tiled=True)
    shells_new = call(
        final_kernel,
        "final",
        f32(new_slots, count, cells),
        [SMEM, SMEM, VMEM, VMEM, VMEM, VMEM] + [ANY] * chips,
        ANY,
        (recv, precv, cap_row, trans_row, inverse, rows, *arrived),
        [
            pltpu.VMEM((chips * CAP, count, cells), jnp.float32),
            pltpu.VMEM((new_slots, count, cells), jnp.float32),
            pltpu.SemaphoreType.DMA((chips,)),
            pltpu.SemaphoreType.DMA((new_slots // 2,)),
        ],
    )
    return (result, shells_new[None])


def solution(mesh):
    placed_at = (
        P("slab", "col"),
        P("slab", "col"),
        P("slab", "col"),
        P("slab", "col"),
        P("col", "slab", None, None),
        P(),
        P(),
        P("col", None),
        P("col", "slab"),
    )
    return jax.shard_map(
        shards,
        mesh=mesh,
        in_specs=placed_at,
        out_specs=(P("slab", "col"), P("col", "slab", None, None)),
        check_vma=False,
    )
```

```python
import functools

import jax
import jax.numpy as jnp
from jax import lax
from jax.experimental import pallas as pl
from jax.experimental.pallas import tpu as pltpu
from jax.sharding import PartitionSpec as P


CAP = 4
STEPS = 2
ITERS = 3
EDGE = 8
LANES = 128
FIELDS = 7
GRANT = 16 * 2**20
FILL = (1.0, 1.0, 0.0, 0.0, 0.0, 0.0, 0.0)


VMEM = pl.BlockSpec(memory_space=pltpu.VMEM)
SMEM = pl.BlockSpec(memory_space=pltpu.SMEM)
ANY = pl.BlockSpec(memory_space=pl.ANY)
HBM = pl.BlockSpec(memory_space=pltpu.HBM)


def iota(shape, dim):
    return lax.broadcasted_iota(jnp.int32, shape, dim)


def split_by(value, size):
    if size & (size - 1) == 0:
        return value >> (size.bit_length() - 1), value & (size - 1)
    return value // size, value % size


def column_of(row, eye):
    return jnp.sum(jnp.where(eye, row, 0.0), axis=1, keepdims=True)


def row_of(column, count):
    eye = iota((count, count), 0) == iota((count, count), 1)
    return jnp.sum(jnp.where(eye, column, 0.0), axis=0, keepdims=True)


def placed(target, value, count):
    width = target.shape[1]
    hit = iota((count, width), 0) == target
    column = jnp.sum(jnp.where(hit, value.astype(jnp.float32), 0.0), axis=1, keepdims=True)
    return row_of(column, count).astype(jnp.int32)


def inverse_of(cap_row, trans_row):
    count = cap_row.shape[1]
    rows, cols = iota((count, count), 0), iota((count, count), 1)
    eye = rows == cols
    cap = column_of(cap_row, eye)
    trans = column_of(trans_row, eye)
    above = column_of(trans_row, cols == rows + 1)
    shape = (count, LANES)
    diag = jnp.broadcast_to(cap + trans + above, shape)
    low = jnp.broadcast_to(jnp.where(iota((count, 1), 0) == 0, 0.0, trans), shape)
    high = jnp.broadcast_to(above, shape)
    rhs = jnp.where(iota(shape, 0) == iota(shape, 1), 1.0, 0.0)
    step = 1
    while step < count:
        down = functools.partial(pltpu.roll, shift=step, axis=0)
        up = functools.partial(pltpu.roll, shift=count - step, axis=0)
        alpha = low / down(diag)
        gamma = high / up(diag)
        diag = diag - alpha * down(high) - gamma * up(low)
        rhs = rhs + alpha * down(rhs) + gamma * up(rhs)
        low, high = alpha * down(low), gamma * up(high)
        step *= 2
    return rhs / diag, cap, trans


def pack_sides(get, rows):
    lane = iota((rows, LANES), 1)
    out = jnp.zeros((rows, LANES), jnp.float32)
    for f in range(FIELDS):
        value = get(f)
        first, last = value[:, :LANES], value[:, -LANES:]
        at = 2 * EDGE * f
        moved = pltpu.roll(first, at, axis=1) if at else first
        out = jnp.where((lane >= at) & (lane < at + EDGE), moved, out)
        moved = pltpu.roll(last, (at + 2 * EDGE) % LANES, axis=1)
        out = jnp.where((lane >= at + EDGE) & (lane < at + 2 * EDGE), moved, out)
    return out


def base_kernel(
    cap_hbm, trans_hbm, table_hbm, block_hbm, shells_hbm, p_hbm, storage_hbm, t_hbm, source_hbm,
    inv_ref, const_ref, slot_ref, place_ref, recv_ref, cap_ref, trans_ref, held,
    p_ref, storage_ref, t_ref, source_ref, b1_ref, b2_ref, e_ref, a_ref, b_ref, side_ref,
    tiles, table_ref, block_row, block_ref, sem, chunk_sem,
):
    me = lax.axis_index("slab")
    slabs = lax.axis_size("slab")
    even = me % 2 == 0
    old_slots, count, _ = shells_hbm.shape
    chunks = 4
    per = old_slots // chunks
    loads = [
        pltpu.make_async_copy(source, target, sem.at[i])
        for i, (source, target) in enumerate((
            (cap_hbm, cap_ref), (trans_hbm, trans_ref), (p_hbm, p_ref), (storage_hbm, storage_ref),
            (t_hbm, t_ref), (source_hbm, source_ref), (table_hbm, table_ref),
            (block_hbm, block_row), (block_hbm, block_ref),
        ))
    ]
    for load in loads:
        load.start()

    def chunk(i):
        part = pl.ds(i * per, per)
        return pltpu.make_async_copy(shells_hbm.at[part], held.at[part], chunk_sem.at[i])

    @pl.when(even)
    def _():
        for i in range(chunks):
            chunk(i).start()

    for load in loads:
        load.wait()
    cap_row, trans_row = cap_ref[...], trans_ref[...]
    inverse, cap, _ = inverse_of(cap_row, trans_row)
    inv_ref[...] = inverse
    t0 = trans_row[:, 0:1]
    first_row = inverse[0:1, :count] * cap_row
    w1 = inverse[:, 0:1] * cap
    w2 = cap * jnp.sum(inverse[:, :count] * first_row, axis=1, keepdims=True)
    couple_row = inverse[0:1, :count] * t0
    c0 = couple_row[:, 0:1]
    c1 = jnp.sum(first_row * couple_row, axis=1, keepdims=True)
    coupling = t0 * (1.0 - c0)
    const_ref[...] = jnp.broadcast_to(t0 * c1 / coupling, const_ref.shape)

    tiles[...] = jnp.zeros_like(tiles)

    @pl.when(even)
    def _():
        v1 = jnp.broadcast_to(t0 * w1, (count, LANES))
        v2 = jnp.broadcast_to(t0 * w2, (count, LANES))
        on = jnp.broadcast_to(coupling, (1, LANES))
        per_row = p_ref.shape[1] // LANES
        for i in range(chunks):
            chunk(i).wait()

            def body(j, carry):
                for u in range(4):
                    slot = i * per + j * 4 + u
                    data = held[slot]
                    row, half = split_by(block_ref[0, slot], per_row)
                    at = pl.ds(row, 1)
                    tiles[0, half, at] = jnp.sum(v1 * data, axis=0, keepdims=True)
                    tiles[1, half, at] = jnp.sum(v2 * data, axis=0, keepdims=True)
                    tiles[2, half, at] = on
                return carry

            lax.fori_loop(0, per // 4, body, 0)

    for i, ref in enumerate((b1_ref, b2_ref, e_ref)):
        ref[...] = jnp.concatenate([tiles[i, h] for h in range(tiles.shape[1])], axis=1)
    fields = (p_ref, storage_ref, t_ref, source_ref, b1_ref, b2_ref, e_ref)
    height = p_ref.shape[0]
    for f, ref in enumerate(fields):
        top, bottom = ref[0:EDGE, :], ref[height - EDGE : height, :]
        a_ref[f] = jnp.where(even, bottom, top)
        b_ref[f] = jnp.where(even, top, bottom)
    side_ref[...] = pack_sides(lambda f: fields[f][...], height)

    table = table_ref[...]
    total = table.shape[1]
    new_slots = total // slabs
    anchor, local = split_by(table, old_slots)
    lane = iota((1, total), 1)
    dest, within = split_by(lane, new_slots)
    rank = jnp.zeros((1, total), jnp.int32)
    for shift in range(1, new_slots):
        same = (pltpu.roll(anchor, shift, axis=1) == anchor) & (within >= shift)
        rank = rank + jnp.where(same, 1, 0)
    rank = jnp.minimum(rank, CAP - 1)
    mine = anchor == me - me % 2
    target = jnp.where(mine, dest * CAP + rank, -1)
    slot_ref[...] = placed(target, local, slabs * CAP)
    eye = iota((old_slots, old_slots), 0) == iota((old_slots, old_slots), 1)
    column = column_of(block_row[...].astype(jnp.float32), eye)
    owner = iota((old_slots, total), 0) == local
    here = jnp.sum(jnp.where(owner, column, 0.0), axis=0, keepdims=True)
    place_ref[...] = placed(target, here, slabs * CAP)
    recv = ((anchor >> 1) ^ (me // 2)) * CAP + rank
    recv_ref[...] = placed(lane - me * new_slots, recv, new_slots)


def pack_kernel(slot_ref, own_ref, other_ref, *out_refs):
    me = lax.axis_index("slab")
    chip, core = me // 2, me % 2
    count = own_ref.shape[1]

    def fill(source):
        for k, ref in enumerate(out_refs):
            for r in range(CAP):
                ref[r, :count] = source[slot_ref[0, ((chip ^ k) * 2 + core) * CAP + r]]

    @pl.when(core == 0)
    def _():
        fill(own_ref)

    @pl.when(core == 1)
    def _():
        fill(other_ref)


def rows_kernel(own_ref, other_ref, *rest):
    near = [ref for ref in rest if len(ref.shape) == 3]
    rest = rest[len(near) // 2 :]
    near, (local, *far) = near[len(near) // 2 :], [ref for ref in rest if len(ref.shape) == 2]
    me = lax.axis_index("slab")
    chip, core = me // 2, me % 2
    for k in range(len(near) + len(far) + 1):
        at = (chip ^ k) * 2 + core
        rows = jnp.where(core == 0, own_ref[at], other_ref[at])
        if k == 0:
            local[...] = rows
        elif k <= len(near):
            ref = near[k - 1]
            ref[0, ref.shape[1] - rows.shape[0] :] = rows
        else:
            far[k - len(near) - 1][...] = rows


def side_kernel(side_ref, a_ref, b_ref, out_ref):
    even = lax.axis_index("slab") % 2 == 0
    height = side_ref.shape[0]
    from_a = pack_sides(lambda f: a_ref[f], EDGE)
    from_b = pack_sides(lambda f: b_ref[f], EDGE)
    out_ref[0:EDGE] = jnp.where(even, from_b, from_a)
    out_ref[EDGE : EDGE + height] = side_ref[...]
    out_ref[EDGE + height :] = jnp.where(even, from_a, from_b)


def fracture_kernel(
    place_ref, const_ref, p_ref, storage_ref, t_ref, source_ref, b1_ref, b2_ref, e_ref,
    a_ref, b_ref, c_ref, d_ref, out_ref, rows_ref, keep,
):
    me, slabs = lax.axis_index("slab"), lax.axis_size("slab")
    col, cols = lax.axis_index("col"), lax.axis_size("col")
    even, col_even = me % 2 == 0, col % 2 == 0
    height, width = p_ref.shape
    tall, wide = height + 2 * EDGE, width + LANES
    row, lane = iota((tall, wide), 0), iota((tall, wide), 1)
    missing = (
        ((me == 0) & (row < EDGE))
        | ((me == slabs - 1) & (row >= EDGE + height))
        | ((lane >= width) & (lane < wide - EDGE) & ((lane >= width + EDGE) | (col == cols - 1)))
        | ((lane >= wide - EDGE) & (col == 0))
    )
    side_lane = iota((tall, LANES), 1)
    right = jnp.where(col_even, c_ref[...], d_ref[...])
    left = jnp.where(col_even, d_ref[...], c_ref[...])
    refs = (p_ref, storage_ref, t_ref, source_ref, b1_ref, b2_ref, e_ref)

    def extended(f):
        top = jnp.where(even, b_ref[f], a_ref[f])
        bottom = jnp.where(even, a_ref[f], b_ref[f])
        own = jnp.concatenate([top, refs[f][...], bottom], axis=0)
        at = 2 * EDGE * f
        from_right = pltpu.roll(right, LANES - at, axis=1) if at else right
        from_left = pltpu.roll(left, LANES - 2 * EDGE - at, axis=1)
        side = jnp.where(side_lane < EDGE, from_right, from_left)
        return jnp.where(missing, FILL[f], jnp.concatenate([own, side], axis=1))

    p, storage, t, source, base1, base2, coef = (extended(f) for f in range(FIELDS))
    next_lane = functools.partial(pltpu.roll, shift=wide - 1, axis=1)
    prev_lane = functools.partial(pltpu.roll, shift=1, axis=1)
    next_row = functools.partial(pltpu.roll, shift=tall - 1, axis=0)
    prev_row = functools.partial(pltpu.roll, shift=1, axis=0)

    def face_of(near):
        total = t + near
        return jnp.where(total > 0.0, 2.0 * t * near / jnp.where(total > 0.0, total, 1.0), 0.0)

    face_h, face_v = face_of(next_lane(t)), face_of(next_row(t))
    conduct = face_h + prev_lane(face_h) + face_v + prev_row(face_v)
    half_h, half_v = face_h * 0.5, face_v * 0.5
    fixed = storage + coef
    rhs = source + base1
    ratio = const_ref[0:1, 0:1]
    for step in range(STEPS):
        prev = p
        for sweep in range(ITERS):
            if sweep == ITERS - 1:
                mid = p[EDGE : EDGE + height]
                for h in range(width // LANES):
                    keep[step, h] = mid[:, h * LANES : (h + 1) * LANES]
                last = p
            near = next_lane(p)
            flow_h = half_h * (near + p) * (near - p)
            near = next_row(p)
            flow_v = half_v * (near + p) * (near - p)
            flux = flow_h - prev_lane(flow_h) + flow_v - prev_row(flow_v)
            misfit = storage * (p - prev) - flux + coef * p - rhs
            p = p - misfit / (fixed + p * conduct)
        rhs = source + base2 + ratio * coef * last
    out_ref[...] = p[EDGE : EDGE + height, :width]

    def body(d, carry):
        for r in range(CAP):
            at_row, half = split_by(place_ref[0, d * CAP + r], width // LANES)
            for step in range(STEPS):
                rows_ref[d, pl.ds(step * CAP + r, 1)] = keep[step, half, pl.ds(at_row, 1)]
        return carry

    lax.fori_loop(0, slabs, body, 0)


def final_kernel(recv_ref, cap_ref, trans_ref, inv_ref, *rest):
    *in_refs, out_ref, held, rows, done, sem = rest
    slots, count = out_ref.shape[:2]
    blocks = [ref for ref in in_refs if len(ref.shape) == 3]
    loose = [ref for ref in in_refs if len(ref.shape) == 2]
    for k, ref in enumerate(blocks):
        held[pl.ds(k * CAP, CAP)] = ref[:, :count]
        inside = ref.shape[1] > count
        rows[k] = ref[0, count:] if inside else loose.pop(0)[...]
    cap_row = cap_ref[...]
    inverse = inv_ref[:, :count]
    t0 = trans_ref[:, 0:1]
    a = inverse * cap_row
    couple = inv_ref[:, 0:1] * t0
    couple2 = jnp.sum(a * (inverse[0:1, :] * t0), axis=1, keepdims=True)
    square = jnp.dot(a, a, preferred_element_type=jnp.float32, precision=lax.Precision.HIGHEST)
    high = square.astype(jnp.bfloat16)
    low = (square - high.astype(jnp.float32)).astype(jnp.bfloat16)
    left = jnp.concatenate([high, high, low], axis=1)
    m1 = jnp.broadcast_to(couple2, (count, LANES))
    m2 = jnp.broadcast_to(couple, (count, LANES))
    pair = 2

    def write(j):
        part = pl.ds(j * pair, pair)
        return pltpu.make_async_copy(done.at[part], out_ref.at[part], sem.at[j])

    for j in range(slots // pair):
        parts = []
        for u in range(pair):
            data = held[recv_ref[0, j * pair + u]]
            hi = data.astype(jnp.bfloat16)
            lo = (data - hi.astype(jnp.float32)).astype(jnp.bfloat16)
            parts.append(jnp.concatenate([hi, lo, hi], axis=0))
        product = jnp.dot(left, jnp.concatenate(parts, axis=1), preferred_element_type=jnp.float32)
        for u in range(pair):
            k, r = split_by(recv_ref[0, j * pair + u], CAP)
            p1 = rows[k, pl.ds(r, 1)]
            p2 = rows[k, pl.ds(r + CAP, 1)]
            done[j * pair + u] = product[:, u * LANES : (u + 1) * LANES] + m1 * p1 + m2 * p2
        write(j).start()
    for j in range(slots // pair):
        write(j).wait()


def call(kernel, out_shape, in_specs, out_specs, args, scratch=(), aliases=None):
    return pl.pallas_call(
        kernel,
        out_shape=out_shape,
        in_specs=in_specs,
        out_specs=out_specs,
        scratch_shapes=scratch,
        input_output_aliases=aliases or {},
        compiler_params=pltpu.CompilerParams(vmem_limit_bytes=GRANT),
    )(*args)


def f32(*shape):
    return jax.ShapeDtypeStruct(shape, jnp.float32)


def i32(*shape):
    return jax.ShapeDtypeStruct(shape, jnp.int32)


def swaps(size, odd):
    if not odd:
        return [(i, i ^ 1) for i in range(size)]
    return [(i, min(max(((i + 1) ^ 1) - 1, 0), size - 1)) for i in range(size)]


def distances(slabs):
    chips = slabs // 2
    return list(range(1, chips // 2)), list(range(chips // 2, chips))


def shards(
    pressure, storage, trans, source, shells_old, shell_cap, shell_trans, new_source, cell_block
):
    slabs, cols = lax.axis_size("slab"), lax.axis_size("col")
    height, width = pressure.shape
    old_slots, count, cells = shells_old.shape[1:]
    new_slots = new_source.shape[1] // slabs
    chips = slabs // 2
    shells = shells_old[0]
    cap_row, trans_row = shell_cap.reshape(1, count), shell_trans.reshape(1, count)

    tall = height + 2 * EDGE
    tail = STEPS * CAP
    near_k, far_k = distances(slabs)

    def chip_swap(value, k):
        return lax.ppermute(value, "slab", [(i, i ^ (2 * k)) for i in range(slabs)])

    hopped = lax.ppermute(shells, "slab", swaps(slabs, False))
    plane, edge = f32(height, width), f32(FIELDS, EDGE, width)
    (
        inverse, const, slot, place, recv, cap_row, trans_row, held,
        pressure, storage, trans, source, base1, base2, coef, edge_a, edge_b, side,
    ) = call(
        base_kernel,
        (
            f32(count, LANES), f32(1, LANES), i32(1, slabs * CAP), i32(1, slabs * CAP),
            i32(1, new_slots), f32(1, count), f32(1, count), f32(old_slots, count, cells),
            *(plane,) * 7, edge, edge, f32(height, LANES),
        ),
        [HBM] * 9,
        (VMEM,) * 18,
        tuple(
            pltpu.with_memory_space_constraint(value, pltpu.HBM)
            for value in (
                cap_row, trans_row, new_source, cell_block, shells, pressure, storage, trans, source
            )
        ),
        [
            pltpu.VMEM((3, width // LANES, height, LANES), jnp.float32),
            pltpu.VMEM(new_source.shape, jnp.int32),
            pltpu.VMEM(cell_block.shape, jnp.int32),
            pltpu.SMEM(cell_block.shape, jnp.int32),
            pltpu.SemaphoreType.DMA((9,)),
            pltpu.SemaphoreType.DMA((4,)),
        ],
    )
    edge_b = lax.ppermute(edge_b, "slab", swaps(slabs, True))
    edge_a = lax.ppermute(edge_a, "slab", swaps(slabs, False))
    packed = call(
        pack_kernel,
        tuple(f32(CAP, count + (tail if k in near_k else 0), cells) for k in range(chips)),
        [SMEM, VMEM, VMEM],
        (VMEM,) * chips,
        (slot, held, hopped),
    )
    side = call(side_kernel, f32(tall, LANES), [VMEM] * 3, VMEM, (side, edge_a, edge_b))
    side_c = lax.ppermute(side, "col", swaps(cols, False))
    side_d = lax.ppermute(side, "col", swaps(cols, True)) if cols > 2 else side_c
    far = [chip_swap(packed[k], k) for k in far_k]

    result, rows = call(
        fracture_kernel,
        (plane, f32(slabs, tail, LANES)),
        [SMEM] + [VMEM] * 12,
        (VMEM, VMEM),
        (
            place, const, pressure, storage, trans, source, base1, base2, coef,
            edge_a, edge_b, side_c, side_d,
        ),
        [pltpu.VMEM((STEPS, width // LANES, height, LANES), jnp.float32)],
    )
    other_rows = lax.ppermute(rows, "slab", swaps(slabs, False))
    filled = call(
        rows_kernel,
        tuple(f32(CAP, count + tail, cells) for k in near_k) + (f32(tail, cells),) * (1 + len(far_k)),
        [VMEM] * (2 + len(near_k)),
        (VMEM,) * chips,
        (rows, other_rows, *(packed[k] for k in near_k)),
        aliases={2 + i: i for i in range(len(near_k))},
    )
    near, (local_rows, *far_rows) = filled[: len(near_k)], filled[len(near_k) :]
    near = [chip_swap(value, k) for value, k in zip(near, near_k)]
    far_rows = [chip_swap(value, k) for value, k in zip(far_rows, far_k)]
    shells_new = call(
        final_kernel,
        f32(new_slots, count, cells),
        [SMEM] + [VMEM] * (3 + chips + 1 + len(far_k)),
        ANY,
        (recv, cap_row, trans_row, inverse, packed[0], *near, *far, local_rows, *far_rows),
        [
            pltpu.VMEM((chips * CAP, count, cells), jnp.float32),
            pltpu.VMEM((chips, tail, cells), jnp.float32),
            pltpu.VMEM((new_slots, count, cells), jnp.float32),
            pltpu.SemaphoreType.DMA((new_slots // 2,)),
        ],
    )
    return (result, shells_new[None])


def solution(mesh):
    placed_at = (
        P("slab", "col"),
        P("slab", "col"),
        P("slab", "col"),
        P("slab", "col"),
        P("col", "slab", None, None),
        P(),
        P(),
        P("col", None),
        P("col", "slab"),
    )
    return jax.shard_map(
        shards,
        mesh=mesh,
        in_specs=placed_at,
        out_specs=(P("slab", "col"), P("col", "slab", None, None)),
        check_vma=False,
    )
```

```python
import functools

import jax
import jax.numpy as jnp
from jax import lax
from jax.experimental import pallas as pl
from jax.experimental.pallas import tpu as pltpu
from jax.sharding import PartitionSpec as P


CAP = 4
STEPS = 2
ITERS = 3
EDGE = 8
LANES = 128
FIELDS = 7
GRANT = 16 * 2**20
FILL = (1.0, 1.0, 0.0, 0.0, 0.0, 0.0, 0.0)


VMEM = pl.BlockSpec(memory_space=pltpu.VMEM)
SMEM = pl.BlockSpec(memory_space=pltpu.SMEM)
ANY = pl.BlockSpec(memory_space=pl.ANY)
HBM = pl.BlockSpec(memory_space=pltpu.HBM)


def iota(shape, dim):
    return lax.broadcasted_iota(jnp.int32, shape, dim)


def split_by(value, size):
    if size & (size - 1) == 0:
        return value >> (size.bit_length() - 1), value & (size - 1)
    return value // size, value % size


def column_of(row, eye):
    return jnp.sum(jnp.where(eye, row, 0.0), axis=1, keepdims=True)


def row_of(column, count):
    eye = iota((count, count), 0) == iota((count, count), 1)
    return jnp.sum(jnp.where(eye, column, 0.0), axis=0, keepdims=True)


def placed(target, value, count):
    width = target.shape[1]
    hit = iota((count, width), 0) == target
    column = jnp.sum(jnp.where(hit, value.astype(jnp.float32), 0.0), axis=1, keepdims=True)
    return row_of(column, count).astype(jnp.int32)


def inverse_of(cap_row, trans_row):
    count = cap_row.shape[1]
    rows, cols = iota((count, count), 0), iota((count, count), 1)
    eye = rows == cols
    cap = column_of(cap_row, eye)
    trans = column_of(trans_row, eye)
    above = column_of(trans_row, cols == rows + 1)
    shape = (count, LANES)
    diag = jnp.broadcast_to(cap + trans + above, shape)
    low = jnp.broadcast_to(jnp.where(iota((count, 1), 0) == 0, 0.0, trans), shape)
    high = jnp.broadcast_to(above, shape)
    rhs = jnp.where(iota(shape, 0) == iota(shape, 1), 1.0, 0.0)
    step = 1
    while step < count:
        down = functools.partial(pltpu.roll, shift=step, axis=0)
        up = functools.partial(pltpu.roll, shift=count - step, axis=0)
        alpha = low / down(diag)
        gamma = high / up(diag)
        diag = diag - alpha * down(high) - gamma * up(low)
        rhs = rhs + alpha * down(rhs) + gamma * up(rhs)
        low, high = alpha * down(low), gamma * up(high)
        step *= 2
    return rhs / diag, cap, trans


def pack_sides(get, rows):
    lane = iota((rows, LANES), 1)
    out = jnp.zeros((rows, LANES), jnp.float32)
    for f in range(FIELDS):
        value = get(f)
        first, last = value[:, :LANES], value[:, -LANES:]
        at = 2 * EDGE * f
        moved = pltpu.roll(first, at, axis=1) if at else first
        out = jnp.where((lane >= at) & (lane < at + EDGE), moved, out)
        moved = pltpu.roll(last, (at + 2 * EDGE) % LANES, axis=1)
        out = jnp.where((lane >= at + EDGE) & (lane < at + 2 * EDGE), moved, out)
    return out


def base_kernel(
    cap_hbm, trans_hbm, table_hbm, block_hbm, shells_hbm, p_hbm, storage_hbm, t_hbm, source_hbm,
    inv_ref, const_ref, slot_ref, place_ref, recv_ref, cap_ref, trans_ref, held,
    p_ref, storage_ref, t_ref, source_ref, b1_ref, b2_ref, e_ref, a_ref, b_ref, side_ref,
    tiles, table_ref, block_row, block_ref, sem, chunk_sem,
):
    me = lax.axis_index("slab")
    slabs = lax.axis_size("slab")
    even = me % 2 == 0
    old_slots, count, _ = shells_hbm.shape
    chunks = 4
    per = old_slots // chunks
    loads = [
        pltpu.make_async_copy(source, target, sem.at[i])
        for i, (source, target) in enumerate((
            (cap_hbm, cap_ref), (trans_hbm, trans_ref), (p_hbm, p_ref), (storage_hbm, storage_ref),
            (t_hbm, t_ref), (source_hbm, source_ref), (table_hbm, table_ref),
            (block_hbm, block_row), (block_hbm, block_ref),
        ))
    ]
    for load in loads:
        load.start()

    def chunk(i):
        part = pl.ds(i * per, per)
        return pltpu.make_async_copy(shells_hbm.at[part], held.at[part], chunk_sem.at[i])

    @pl.when(even)
    def _():
        for i in range(chunks):
            chunk(i).start()

    for load in loads:
        load.wait()
    cap_row, trans_row = cap_ref[...], trans_ref[...]
    inverse, cap, _ = inverse_of(cap_row, trans_row)
    inv_ref[...] = inverse
    t0 = trans_row[:, 0:1]
    first_row = inverse[0:1, :count] * cap_row
    w1 = inverse[:, 0:1] * cap
    w2 = cap * jnp.sum(inverse[:, :count] * first_row, axis=1, keepdims=True)
    couple_row = inverse[0:1, :count] * t0
    c0 = couple_row[:, 0:1]
    c1 = jnp.sum(first_row * couple_row, axis=1, keepdims=True)
    coupling = t0 * (1.0 - c0)
    const_ref[...] = jnp.broadcast_to(t0 * c1 / coupling, const_ref.shape)

    tiles[...] = jnp.zeros_like(tiles)

    @pl.when(even)
    def _():
        v1 = jnp.broadcast_to(t0 * w1, (count, LANES))
        v2 = jnp.broadcast_to(t0 * w2, (count, LANES))
        on = jnp.broadcast_to(coupling, (1, LANES))
        per_row = p_ref.shape[1] // LANES
        for i in range(chunks):
            chunk(i).wait()

            def body(j, carry):
                for u in range(4):
                    slot = i * per + j * 4 + u
                    data = held[slot]
                    row, half = split_by(block_ref[0, slot], per_row)
                    at = pl.ds(row, 1)
                    tiles[0, half, at] = jnp.sum(v1 * data, axis=0, keepdims=True)
                    tiles[1, half, at] = jnp.sum(v2 * data, axis=0, keepdims=True)
                    tiles[2, half, at] = on
                return carry

            lax.fori_loop(0, per // 4, body, 0)

    for i, ref in enumerate((b1_ref, b2_ref, e_ref)):
        ref[...] = jnp.concatenate([tiles[i, h] for h in range(tiles.shape[1])], axis=1)
    fields = (p_ref, storage_ref, t_ref, source_ref, b1_ref, b2_ref, e_ref)
    height = p_ref.shape[0]
    for f, ref in enumerate(fields):
        top, bottom = ref[0:EDGE, :], ref[height - EDGE : height, :]
        a_ref[f] = jnp.where(even, bottom, top)
        b_ref[f] = jnp.where(even, top, bottom)
    side_ref[...] = pack_sides(lambda f: fields[f][...], height)

    table = table_ref[...]
    total = table.shape[1]
    new_slots = total // slabs
    anchor, local = split_by(table, old_slots)
    lane = iota((1, total), 1)
    dest, within = split_by(lane, new_slots)
    rank = jnp.zeros((1, total), jnp.int32)
    for shift in range(1, new_slots):
        same = (pltpu.roll(anchor, shift, axis=1) == anchor) & (within >= shift)
        rank = rank + jnp.where(same, 1, 0)
    rank = jnp.minimum(rank, CAP - 1)
    mine = anchor == me - me % 2
    target = jnp.where(mine, dest * CAP + rank, -1)
    slot_ref[...] = placed(target, local, slabs * CAP)
    eye = iota((old_slots, old_slots), 0) == iota((old_slots, old_slots), 1)
    column = column_of(block_row[...].astype(jnp.float32), eye)
    owner = iota((old_slots, total), 0) == local
    here = jnp.sum(jnp.where(owner, column, 0.0), axis=0, keepdims=True)
    place_ref[...] = placed(target, here, slabs * CAP)
    recv = ((anchor >> 1) ^ (me // 2)) * CAP + rank
    recv_ref[...] = placed(lane - me * new_slots, recv, new_slots)


def pack_kernel(slot_ref, own_ref, other_ref, *out_refs):
    me = lax.axis_index("slab")
    chip, core = me // 2, me % 2
    count = own_ref.shape[1]

    def fill(source):
        for k, ref in enumerate(out_refs):
            for r in range(CAP):
                ref[r, :count] = source[slot_ref[0, ((chip ^ k) * 2 + core) * CAP + r]]

    @pl.when(core == 0)
    def _():
        fill(own_ref)

    @pl.when(core == 1)
    def _():
        fill(other_ref)


def rows_kernel(late_k, early_k, own_ref, other_ref, *rest):
    local_ref, *outs = rest[len(late_k) :]
    me = lax.axis_index("slab")

    def rows(k):
        at = ((me // 2) ^ k) * 2 + me % 2
        return jnp.where(me % 2 == 0, own_ref[at], other_ref[at])

    local_ref[...] = rows(0)
    for k, ref in zip(late_k, outs):
        value = rows(k)
        ref[0, ref.shape[1] - value.shape[0] :] = value
    for k, ref in zip(early_k, outs[len(late_k) :]):
        ref[...] = rows(k)


def side_kernel(side_ref, a_ref, b_ref, out_ref):
    even = lax.axis_index("slab") % 2 == 0
    height = side_ref.shape[0]
    from_a = pack_sides(lambda f: a_ref[f], EDGE)
    from_b = pack_sides(lambda f: b_ref[f], EDGE)
    out_ref[0:EDGE] = jnp.where(even, from_b, from_a)
    out_ref[EDGE : EDGE + height] = side_ref[...]
    out_ref[EDGE + height :] = jnp.where(even, from_a, from_b)


def fracture_kernel(
    place_ref, const_ref, p_ref, storage_ref, t_ref, source_ref, b1_ref, b2_ref, e_ref,
    a_ref, b_ref, c_ref, d_ref, out_ref, rows_ref, keep,
):
    me, slabs = lax.axis_index("slab"), lax.axis_size("slab")
    col, cols = lax.axis_index("col"), lax.axis_size("col")
    even, col_even = me % 2 == 0, col % 2 == 0
    height, width = p_ref.shape
    tall, wide = height + 2 * EDGE, width + LANES
    row, lane = iota((tall, wide), 0), iota((tall, wide), 1)
    missing = (
        ((me == 0) & (row < EDGE))
        | ((me == slabs - 1) & (row >= EDGE + height))
        | ((lane >= width) & (lane < wide - EDGE) & ((lane >= width + EDGE) | (col == cols - 1)))
        | ((lane >= wide - EDGE) & (col == 0))
    )
    side_lane = iota((tall, LANES), 1)
    right = jnp.where(col_even, c_ref[...], d_ref[...])
    left = jnp.where(col_even, d_ref[...], c_ref[...])
    refs = (p_ref, storage_ref, t_ref, source_ref, b1_ref, b2_ref, e_ref)

    def extended(f):
        top = jnp.where(even, b_ref[f], a_ref[f])
        bottom = jnp.where(even, a_ref[f], b_ref[f])
        own = jnp.concatenate([top, refs[f][...], bottom], axis=0)
        at = 2 * EDGE * f
        from_right = pltpu.roll(right, LANES - at, axis=1) if at else right
        from_left = pltpu.roll(left, LANES - 2 * EDGE - at, axis=1)
        side = jnp.where(side_lane < EDGE, from_right, from_left)
        return jnp.where(missing, FILL[f], jnp.concatenate([own, side], axis=1))

    p, storage, t, source, base1, base2, coef = (extended(f) for f in range(FIELDS))
    next_lane = functools.partial(pltpu.roll, shift=wide - 1, axis=1)
    prev_lane = functools.partial(pltpu.roll, shift=1, axis=1)
    next_row = functools.partial(pltpu.roll, shift=tall - 1, axis=0)
    prev_row = functools.partial(pltpu.roll, shift=1, axis=0)

    def face_of(near):
        total = t + near
        return jnp.where(total > 0.0, 2.0 * t * near / jnp.where(total > 0.0, total, 1.0), 0.0)

    face_h, face_v = face_of(next_lane(t)), face_of(next_row(t))
    conduct = face_h + prev_lane(face_h) + face_v + prev_row(face_v)
    half_h, half_v = face_h * 0.5, face_v * 0.5
    fixed = storage + coef
    rhs = source + base1
    ratio = const_ref[0:1, 0:1]
    for step in range(STEPS):
        prev = p
        for sweep in range(ITERS):
            if sweep == ITERS - 1:
                mid = p[EDGE : EDGE + height]
                for h in range(width // LANES):
                    keep[step, h] = mid[:, h * LANES : (h + 1) * LANES]
                last = p
            near = next_lane(p)
            flow_h = half_h * (near + p) * (near - p)
            near = next_row(p)
            flow_v = half_v * (near + p) * (near - p)
            flux = flow_h - prev_lane(flow_h) + flow_v - prev_row(flow_v)
            misfit = storage * (p - prev) - flux + coef * p - rhs
            p = p - misfit / (fixed + p * conduct)
        rhs = source + base2 + ratio * coef * last
    out_ref[...] = p[EDGE : EDGE + height, :width]

    def body(d, carry):
        for r in range(CAP):
            at_row, half = split_by(place_ref[0, d * CAP + r], width // LANES)
            for step in range(STEPS):
                rows_ref[d, pl.ds(step * CAP + r, 1)] = keep[step, half, pl.ds(at_row, 1)]
        return carry

    lax.fori_loop(0, slabs, body, 0)


def final_kernel(recv_ref, cap_ref, trans_ref, inv_ref, *rest):
    *in_refs, out_ref, held, rows, done, sem = rest
    slots, count = out_ref.shape[:2]
    blocks = [ref for ref in in_refs if len(ref.shape) == 3]
    loose = [ref for ref in in_refs if len(ref.shape) == 2]
    for k, ref in enumerate(blocks):
        held[pl.ds(k * CAP, CAP)] = ref[:, :count]
        inside = ref.shape[1] > count
        rows[k] = ref[0, count:] if inside else loose.pop(0)[...]
    cap_row = cap_ref[...]
    inverse = inv_ref[:, :count]
    t0 = trans_ref[:, 0:1]
    a = inverse * cap_row
    couple = inv_ref[:, 0:1] * t0
    couple2 = jnp.sum(a * (inverse[0:1, :] * t0), axis=1, keepdims=True)
    square = jnp.dot(a, a, preferred_element_type=jnp.float32, precision=lax.Precision.HIGHEST)
    high = square.astype(jnp.bfloat16)
    low = (square - high.astype(jnp.float32)).astype(jnp.bfloat16)
    left = jnp.concatenate([high, high, low], axis=1)
    m1 = jnp.broadcast_to(couple2, (count, LANES))
    m2 = jnp.broadcast_to(couple, (count, LANES))
    pair = 2

    def write(j):
        part = pl.ds(j * pair, pair)
        return pltpu.make_async_copy(done.at[part], out_ref.at[part], sem.at[j])

    for j in range(slots // pair):
        parts = []
        for u in range(pair):
            data = held[recv_ref[0, j * pair + u]]
            hi = data.astype(jnp.bfloat16)
            lo = (data - hi.astype(jnp.float32)).astype(jnp.bfloat16)
            parts.append(jnp.concatenate([hi, lo, hi], axis=0))
        product = jnp.dot(left, jnp.concatenate(parts, axis=1), preferred_element_type=jnp.float32)
        for u in range(pair):
            k, r = split_by(recv_ref[0, j * pair + u], CAP)
            p1 = rows[k, pl.ds(r, 1)]
            p2 = rows[k, pl.ds(r + CAP, 1)]
            done[j * pair + u] = product[:, u * LANES : (u + 1) * LANES] + m1 * p1 + m2 * p2
        write(j).start()
    for j in range(slots // pair):
        write(j).wait()


def call(kernel, out_shape, in_specs, out_specs, args, scratch=(), aliases=None):
    return pl.pallas_call(
        kernel,
        out_shape=out_shape,
        in_specs=in_specs,
        out_specs=out_specs,
        scratch_shapes=scratch,
        input_output_aliases=aliases or {},
        compiler_params=pltpu.CompilerParams(vmem_limit_bytes=GRANT),
    )(*args)


def f32(*shape):
    return jax.ShapeDtypeStruct(shape, jnp.float32)


def i32(*shape):
    return jax.ShapeDtypeStruct(shape, jnp.int32)


def shifts(size):
    return [
        (i, i + 2 if i + 2 < size else i - 1) if i % 2 else (i, i - 2 if i >= 2 else i + 1)
        for i in range(size)
    ]


def swaps(size, odd):
    if not odd:
        return [(i, i ^ 1) for i in range(size)]
    return [(i, min(max(((i + 1) ^ 1) - 1, 0), size - 1)) for i in range(size)]


def distances(slabs):
    chips = slabs // 2
    early = range(chips // 2, chips - max(1, chips // 8))
    return [k for k in range(1, chips) if k not in early], list(early)


def shards(
    pressure, storage, trans, source, shells_old, shell_cap, shell_trans, new_source, cell_block
):
    slabs, cols = lax.axis_size("slab"), lax.axis_size("col")
    height, width = pressure.shape
    old_slots, count, cells = shells_old.shape[1:]
    new_slots = new_source.shape[1] // slabs
    chips = slabs // 2
    shells = shells_old[0]
    cap_row, trans_row = shell_cap.reshape(1, count), shell_trans.reshape(1, count)

    tall = height + 2 * EDGE
    tail = STEPS * CAP
    late_k, early_k = distances(slabs)

    def chip_swap(value, k):
        return lax.ppermute(value, "slab", [(i, i ^ (2 * k)) for i in range(slabs)])

    hopped = lax.ppermute(shells, "slab", swaps(slabs, False))
    plane, edge = f32(height, width), f32(FIELDS, EDGE, width)
    (
        inverse, const, slot, place, recv, cap_row, trans_row, held,
        pressure, storage, trans, source, base1, base2, coef, edge_a, edge_b, side,
    ) = call(
        base_kernel,
        (
            f32(count, LANES), f32(1, LANES), i32(1, slabs * CAP), i32(1, slabs * CAP),
            i32(1, new_slots), f32(1, count), f32(1, count), f32(old_slots, count, cells),
            *(plane,) * 7, edge, edge, f32(height, LANES),
        ),
        [HBM] * 9,
        (VMEM,) * 18,
        tuple(
            pltpu.with_memory_space_constraint(value, pltpu.HBM)
            for value in (
                cap_row, trans_row, new_source, cell_block, shells, pressure, storage, trans, source
            )
        ),
        [
            pltpu.VMEM((3, width // LANES, height, LANES), jnp.float32),
            pltpu.VMEM(new_source.shape, jnp.int32),
            pltpu.VMEM(cell_block.shape, jnp.int32),
            pltpu.SMEM(cell_block.shape, jnp.int32),
            pltpu.SemaphoreType.DMA((9,)),
            pltpu.SemaphoreType.DMA((4,)),
        ],
    )
    edge_b = lax.ppermute(edge_b, "slab", shifts(slabs))
    edge_b = lax.ppermute(edge_b, "slab", swaps(slabs, False))
    edge_a = lax.ppermute(edge_a, "slab", swaps(slabs, False))
    packed = call(
        pack_kernel,
        tuple(f32(CAP, count + (tail if k in late_k else 0), cells) for k in range(chips)),
        [SMEM, VMEM, VMEM],
        (VMEM,) * chips,
        (slot, held, hopped),
    )
    side = call(side_kernel, f32(tall, LANES), [VMEM] * 3, VMEM, (side, edge_a, edge_b))
    side_c = lax.ppermute(side, "col", swaps(cols, False))
    side_d = lax.ppermute(side, "col", swaps(cols, True)) if cols > 2 else side_c
    blocks = {0: packed[0]}
    for k in early_k:
        blocks[k] = chip_swap(packed[k], k)

    result, rows = call(
        fracture_kernel,
        (plane, f32(slabs, tail, LANES)),
        [SMEM] + [VMEM] * 12,
        (VMEM, VMEM),
        (
            place, const, pressure, storage, trans, source, base1, base2, coef,
            edge_a, edge_b, side_c, side_d,
        ),
        [pltpu.VMEM((STEPS, width // LANES, height, LANES), jnp.float32)],
    )
    other_rows = lax.ppermute(rows, "slab", swaps(slabs, False))
    local_rows, *filled = call(
        functools.partial(rows_kernel, late_k, early_k),
        (f32(tail, cells),)
        + (f32(CAP, count + tail, cells),) * len(late_k)
        + (f32(tail, cells),) * len(early_k),
        [VMEM] * (2 + len(late_k)),
        (VMEM,) * chips,
        (rows, other_rows, *(packed[k] for k in late_k)),
        aliases={2 + i: 1 + i for i in range(len(late_k))},
    )
    for k, value in zip(late_k, filled):
        blocks[k] = chip_swap(value, k)
    loose = [chip_swap(value, k) for k, value in zip(early_k, filled[len(late_k) :])]
    shells_new = call(
        final_kernel,
        f32(new_slots, count, cells),
        [SMEM] + [VMEM] * (3 + chips + 1 + len(early_k)),
        ANY,
        (recv, cap_row, trans_row, inverse, *(blocks[k] for k in range(chips)), local_rows, *loose),
        [
            pltpu.VMEM((chips * CAP, count, cells), jnp.float32),
            pltpu.VMEM((chips, tail, cells), jnp.float32),
            pltpu.VMEM((new_slots, count, cells), jnp.float32),
            pltpu.SemaphoreType.DMA((new_slots // 2,)),
        ],
    )
    return (result, shells_new[None])


def solution(mesh):
    placed_at = (
        P("slab", "col"),
        P("slab", "col"),
        P("slab", "col"),
        P("slab", "col"),
        P("col", "slab", None, None),
        P(),
        P(),
        P("col", None),
        P("col", "slab"),
    )
    return jax.shard_map(
        shards,
        mesh=mesh,
        in_specs=placed_at,
        out_specs=(P("slab", "col"), P("col", "slab", None, None)),
        check_vma=False,
    )
```

```python
import functools

import jax
import jax.numpy as jnp
from jax import lax
from jax.experimental import pallas as pl
from jax.experimental.pallas import tpu as pltpu
from jax.sharding import PartitionSpec as P


CAP = 4
STEPS = 2
ITERS = 3
EDGE = 8
LANES = 128
FIELDS = 7
GRANT = 16 * 2**20
FILL = (1.0, 1.0, 0.0, 0.0, 0.0, 0.0, 0.0)


VMEM = pl.BlockSpec(memory_space=pltpu.VMEM)
SMEM = pl.BlockSpec(memory_space=pltpu.SMEM)
ANY = pl.BlockSpec(memory_space=pl.ANY)
HBM = pl.BlockSpec(memory_space=pltpu.HBM)


def iota(shape, dim):
    return lax.broadcasted_iota(jnp.int32, shape, dim)


def split_by(value, size):
    if size & (size - 1) == 0:
        return value >> (size.bit_length() - 1), value & (size - 1)
    return value // size, value % size


def column_of(row, eye):
    return jnp.sum(jnp.where(eye, row, 0.0), axis=1, keepdims=True)


def row_of(column, count):
    eye = iota((count, count), 0) == iota((count, count), 1)
    return jnp.sum(jnp.where(eye, column, 0.0), axis=0, keepdims=True)


def placed(target, value, count):
    width = target.shape[1]
    hit = iota((count, width), 0) == target
    column = jnp.sum(jnp.where(hit, value.astype(jnp.float32), 0.0), axis=1, keepdims=True)
    return row_of(column, count).astype(jnp.int32)


def inverse_of(cap_row, trans_row):
    count = cap_row.shape[1]
    rows, cols = iota((count, count), 0), iota((count, count), 1)
    eye = rows == cols
    cap = column_of(cap_row, eye)
    trans = column_of(trans_row, eye)
    above = column_of(trans_row, cols == rows + 1)
    shape = (count, LANES)
    diag = jnp.broadcast_to(cap + trans + above, shape)
    low = jnp.broadcast_to(jnp.where(iota((count, 1), 0) == 0, 0.0, trans), shape)
    high = jnp.broadcast_to(above, shape)
    rhs = jnp.where(iota(shape, 0) == iota(shape, 1), 1.0, 0.0)
    step = 1
    while step < count:
        down = functools.partial(pltpu.roll, shift=step, axis=0)
        up = functools.partial(pltpu.roll, shift=count - step, axis=0)
        alpha = low / down(diag)
        gamma = high / up(diag)
        diag = diag - alpha * down(high) - gamma * up(low)
        rhs = rhs + alpha * down(rhs) + gamma * up(rhs)
        low, high = alpha * down(low), gamma * up(high)
        step *= 2
    return rhs / diag, cap


def sent_blocks(table, old_slots, slabs):
    me = lax.axis_index("slab")
    total = table.shape[1]
    new_slots = total // slabs
    anchor, local = split_by(table, old_slots)
    dest, within = split_by(iota((1, total), 1), new_slots)
    mine = anchor == me - me % 2
    seen = jnp.where(mine, 1, 0)
    shift = 1
    while shift < new_slots:
        seen = seen + jnp.where(within >= shift, pltpu.roll(seen, shift, axis=1), 0)
        shift *= 2
    return jnp.where(mine, dest * CAP + jnp.minimum(seen, CAP) - 1, -1), local


def pack_sides(get, rows):
    lane = iota((rows, LANES), 1)
    out = jnp.zeros((rows, LANES), jnp.float32)
    for f in range(FIELDS):
        value = get(f)
        first, last = value[:, :LANES], value[:, -LANES:]
        at = 2 * EDGE * f
        moved = pltpu.roll(first, at, axis=1) if at else first
        out = jnp.where((lane >= at) & (lane < at + EDGE), moved, out)
        moved = pltpu.roll(last, (at + 2 * EDGE) % LANES, axis=1)
        out = jnp.where((lane >= at + EDGE) & (lane < at + 2 * EDGE), moved, out)
    return out


def base_kernel(
    cap_hbm, trans_hbm, table_hbm, block_hbm, shells_hbm, p_hbm, storage_hbm, t_hbm, source_hbm,
    inv_ref, const_ref, slot_ref, table_ref, block_row, cap_ref, trans_ref, held,
    p_ref, storage_ref, t_ref, source_ref, b1_ref, b2_ref, e_ref, a_ref, b_ref,
    tiles, block_ref, sem, chunk_sem,
):
    me = lax.axis_index("slab")
    slabs = lax.axis_size("slab")
    even = me % 2 == 0
    old_slots, count, _ = shells_hbm.shape
    chunks = 4
    per = old_slots // chunks
    loads = [
        pltpu.make_async_copy(source, target, sem.at[i])
        for i, (source, target) in enumerate((
            (cap_hbm, cap_ref), (trans_hbm, trans_ref), (p_hbm, p_ref), (storage_hbm, storage_ref),
            (t_hbm, t_ref), (source_hbm, source_ref), (table_hbm, table_ref),
            (block_hbm, block_row), (block_hbm, block_ref),
        ))
    ]
    for load in loads:
        load.start()

    def chunk(i):
        part = pl.ds(i * per, per)
        return pltpu.make_async_copy(shells_hbm.at[part], held.at[part], chunk_sem.at[i])

    @pl.when(even)
    def _():
        for i in range(chunks):
            chunk(i).start()

    for load in loads:
        load.wait()
    cap_row, trans_row = cap_ref[...], trans_ref[...]
    inverse, cap = inverse_of(cap_row, trans_row)
    inv_ref[...] = inverse
    t0 = trans_row[:, 0:1]
    first_row = inverse[0:1, :count] * cap_row
    w1 = inverse[:, 0:1] * cap
    w2 = cap * jnp.sum(inverse[:, :count] * first_row, axis=1, keepdims=True)
    couple_row = inverse[0:1, :count] * t0
    c0 = couple_row[:, 0:1]
    c1 = jnp.sum(first_row * couple_row, axis=1, keepdims=True)
    coupling = t0 * (1.0 - c0)
    const_ref[...] = jnp.broadcast_to(t0 * c1 / coupling, const_ref.shape)

    tiles[...] = jnp.zeros_like(tiles)

    @pl.when(even)
    def _():
        v1 = jnp.broadcast_to(t0 * w1, (count, LANES))
        v2 = jnp.broadcast_to(t0 * w2, (count, LANES))
        on = jnp.broadcast_to(coupling, (1, LANES))
        per_row = p_ref.shape[1] // LANES
        for i in range(chunks):
            chunk(i).wait()

            for slot in range(i * per, (i + 1) * per):
                data = held[slot]
                row, half = split_by(block_ref[0, slot], per_row)
                at = pl.ds(row, 1)
                tiles[0, half, at] = jnp.sum(v1 * data, axis=0, keepdims=True)
                tiles[1, half, at] = jnp.sum(v2 * data, axis=0, keepdims=True)
                tiles[2, half, at] = on

    for i, ref in enumerate((b1_ref, b2_ref, e_ref)):
        ref[...] = jnp.concatenate([tiles[i, h] for h in range(tiles.shape[1])], axis=1)
    fields = (p_ref, storage_ref, t_ref, source_ref, b1_ref, b2_ref, e_ref)
    height = p_ref.shape[0]
    for f, ref in enumerate(fields):
        top, bottom = ref[0:EDGE, :], ref[height - EDGE : height, :]
        a_ref[f] = jnp.where(even, bottom, top)
        b_ref[f] = jnp.where(even, top, bottom)
    target, local = sent_blocks(table_ref[...], old_slots, slabs)
    slot_ref[...] = placed(target, local, slabs * CAP)


def pack_kernel(slot_ref, own_ref, other_ref, *out_refs):
    me = lax.axis_index("slab")
    chip, core = me // 2, me % 2
    count = own_ref.shape[1]

    def fill(source):
        for k, ref in enumerate(out_refs):
            for r in range(CAP):
                ref[r, :count] = source[slot_ref[0, ((chip ^ k) * 2 + core) * CAP + r]]

    @pl.when(core == 0)
    def _():
        fill(own_ref)

    @pl.when(core == 1)
    def _():
        fill(other_ref)


def rows_kernel(late_k, early_k, own_ref, other_ref, *rest):
    local_ref, *outs = rest[len(late_k) :]
    me = lax.axis_index("slab")

    def rows(k):
        at = ((me // 2) ^ k) * 2 + me % 2
        return jnp.where(me % 2 == 0, own_ref[at], other_ref[at])

    local_ref[...] = rows(0)
    for k, ref in zip(late_k, outs):
        value = rows(k)
        ref[0, ref.shape[1] - value.shape[0] :] = value
    for k, ref in zip(early_k, outs[len(late_k) :]):
        ref[...] = rows(k)


def side_kernel(table_ref, block_ref, *rest):
    *fields, a_ref, b_ref, out_ref, place_ref, recv_ref = rest
    me, slabs = lax.axis_index("slab"), lax.axis_size("slab")
    even = me % 2 == 0
    height = fields[0].shape[0]
    from_a = pack_sides(lambda f: a_ref[f], EDGE)
    from_b = pack_sides(lambda f: b_ref[f], EDGE)
    out_ref[0:EDGE] = jnp.where(even, from_b, from_a)
    out_ref[EDGE : EDGE + height] = pack_sides(lambda f: fields[f][...], height)
    out_ref[EDGE + height :] = jnp.where(even, from_a, from_b)

    old_slots = block_ref.shape[1]
    table = table_ref[...]
    total = table.shape[1]
    target, local = sent_blocks(table, old_slots, slabs)
    eye = iota((old_slots, old_slots), 0) == iota((old_slots, old_slots), 1)
    column = column_of(block_ref[...].astype(jnp.float32), eye)
    owner = iota((old_slots, total), 0) == local
    here = jnp.sum(jnp.where(owner, column, 0.0), axis=0, keepdims=True)
    place_ref[...] = placed(target, here, slabs * CAP)

    count = recv_ref.shape[1]
    anchor, _ = split_by(placed(iota((1, total), 1) - me * count, table, count), old_slots)
    row, above = iota((count, count), 0), iota((count, count), 1)
    column = column_of(anchor.astype(jnp.float32), row == above)
    same = (column == anchor.astype(jnp.float32)) & (above < row)
    rank = row_of(jnp.sum(jnp.where(same, 1.0, 0.0), axis=1, keepdims=True), count)
    rank = jnp.minimum(rank.astype(jnp.int32), CAP - 1)
    recv_ref[...] = ((anchor >> 1) ^ (me // 2)) * CAP + rank


def fracture_kernel(
    place_ref, const_ref, p_ref, storage_ref, t_ref, source_ref, b1_ref, b2_ref, e_ref,
    a_ref, b_ref, c_ref, d_ref, out_ref, rows_ref, keep, place, sem,
):
    table = pltpu.make_async_copy(place_ref, place, sem)
    table.start()
    me, slabs = lax.axis_index("slab"), lax.axis_size("slab")
    col, cols = lax.axis_index("col"), lax.axis_size("col")
    even, col_even = me % 2 == 0, col % 2 == 0
    height, width = p_ref.shape
    tall, wide = height + 2 * EDGE, width + LANES
    row, lane = iota((tall, wide), 0), iota((tall, wide), 1)
    missing = (
        ((me == 0) & (row < EDGE))
        | ((me == slabs - 1) & (row >= EDGE + height))
        | ((lane >= width) & (lane < wide - EDGE) & ((lane >= width + EDGE) | (col == cols - 1)))
        | ((lane >= wide - EDGE) & (col == 0))
    )
    side_lane = iota((tall, LANES), 1)
    right = jnp.where(col_even, c_ref[...], d_ref[...])
    left = jnp.where(col_even, d_ref[...], c_ref[...])
    refs = (p_ref, storage_ref, t_ref, source_ref, b1_ref, b2_ref, e_ref)

    def extended(f):
        top = jnp.where(even, b_ref[f], a_ref[f])
        bottom = jnp.where(even, a_ref[f], b_ref[f])
        own = jnp.concatenate([top, refs[f][...], bottom], axis=0)
        at = 2 * EDGE * f
        from_right = pltpu.roll(right, LANES - at, axis=1) if at else right
        from_left = pltpu.roll(left, LANES - 2 * EDGE - at, axis=1)
        side = jnp.where(side_lane < EDGE, from_right, from_left)
        return jnp.where(missing, FILL[f], jnp.concatenate([own, side], axis=1))

    p, storage, t, source, base1, base2, coef = (extended(f) for f in range(FIELDS))
    next_lane = functools.partial(pltpu.roll, shift=wide - 1, axis=1)
    prev_lane = functools.partial(pltpu.roll, shift=1, axis=1)
    next_row = functools.partial(pltpu.roll, shift=tall - 1, axis=0)
    prev_row = functools.partial(pltpu.roll, shift=1, axis=0)

    def face_of(near):
        total = t + near
        return jnp.where(total > 0.0, 2.0 * t * near / jnp.where(total > 0.0, total, 1.0), 0.0)

    face_h, face_v = face_of(next_lane(t)), face_of(next_row(t))
    conduct = face_h + prev_lane(face_h) + face_v + prev_row(face_v)
    half_h, half_v = face_h * 0.5, face_v * 0.5
    fixed = storage + coef
    rhs = source + base1
    ratio = const_ref[0:1, 0:1]
    for step in range(STEPS):
        prev = p
        for sweep in range(ITERS):
            if sweep == ITERS - 1:
                mid = p[EDGE : EDGE + height]
                for h in range(width // LANES):
                    keep[step, h] = mid[:, h * LANES : (h + 1) * LANES]
                last = p
            square = p * p
            if step == STEPS - 1 and sweep == ITERS - 1:
                break
            flow_h = half_h * (next_lane(square) - square)
            flow_v = half_v * (next_row(square) - square)
            flux = flow_h - prev_lane(flow_h) + flow_v - prev_row(flow_v)
            misfit = storage * (p - prev) - flux + coef * p - rhs
            p = p - misfit / (fixed + p * conduct)
        if step < STEPS - 1:
            rhs = source + base2 + ratio * coef * last

    def own(value):
        return value[EDGE : EDGE + height, :width]

    strip, slab = square[EDGE : EDGE + height], square[:, :width]
    flow_h = half_h[EDGE : EDGE + height] * (next_lane(strip) - strip)
    flow_v = half_v[:, :width] * (next_row(slab) - slab)
    flux = (flow_h - prev_lane(flow_h))[:, :width] + (flow_v - prev_row(flow_v))[EDGE : EDGE + height]
    p, prev = own(p), own(prev)
    misfit = own(storage) * (p - prev) - flux + own(coef) * p - own(rhs)
    out_ref[...] = p - misfit / (own(fixed) + p * own(conduct))

    table.wait()
    for q in range(rows_ref.shape[0] * CAP):
        d, r = q // CAP, q % CAP
        at_row, half = split_by(place[0, q], width // LANES)
        for step in range(STEPS):
            rows_ref[d, pl.ds(step * CAP + r, 1)] = keep[step, half, pl.ds(at_row, 1)]


def multiply(left, blocks):
    results = []
    for first in range(0, len(blocks), 2):
        parts = []
        for data in blocks[first : first + 2]:
            hi = data.astype(jnp.bfloat16)
            lo = (data - hi.astype(jnp.float32)).astype(jnp.bfloat16)
            parts.append(jnp.concatenate([hi, lo, hi], axis=0))
        product = jnp.dot(left, jnp.concatenate(parts, axis=1), preferred_element_type=jnp.float32)
        results += [product[:, :LANES], product[:, LANES:]]
    return results


def product_kernel(cap_ref, trans_ref, inv_ref, *rest):
    *blocks, left_ref, m_ref, out_ref = rest
    count = cap_ref.shape[1]
    inverse = inv_ref[:, :count]
    t0 = trans_ref[:, 0:1]
    a = inverse * cap_ref[...]
    couple = inv_ref[:, 0:1] * t0
    couple2 = jnp.sum(a * (inverse[0:1, :] * t0), axis=1, keepdims=True)
    square = jnp.dot(a, a, preferred_element_type=jnp.float32, precision=lax.Precision.HIGHEST)
    high = square.astype(jnp.bfloat16)
    low = (square - high.astype(jnp.float32)).astype(jnp.bfloat16)
    left = jnp.concatenate([high, high, low], axis=1)
    left_ref[...] = left
    m_ref[0] = jnp.broadcast_to(couple2, (count, LANES))
    m_ref[1] = jnp.broadcast_to(couple, (count, LANES))
    for i, ref in enumerate(blocks):
        for r, value in enumerate(multiply(left, [ref[r, :count] for r in range(CAP)])):
            out_ref[i * CAP + r] = value


def final_kernel(ready_k, tailed_k, loose_k, recv_ref, left_ref, m_ref, product_ref, *rest):
    *in_refs, out_ref, held, rows, done, recv, recv_sem, sem = rest
    slots, count = out_ref.shape[:2]
    table = pltpu.make_async_copy(recv_ref, recv, recv_sem)
    table.start()
    for i, k in enumerate(ready_k):
        held[pl.ds(k * CAP, CAP)] = product_ref[pl.ds(i * CAP, CAP)]
    left = left_ref[...]
    for k, ref in zip(tailed_k, in_refs):
        rows[k] = ref[0, count:]
        if k not in ready_k:
            for r, value in enumerate(multiply(left, [ref[r, :count] for r in range(CAP)])):
                held[k * CAP + r] = value
    for k, ref in zip(loose_k, in_refs[len(tailed_k) :]):
        rows[k] = ref[...]
    m1, m2 = m_ref[0], m_ref[1]
    group = 4
    table.wait()

    def write(j):
        part = pl.ds(j * group, group)
        return pltpu.make_async_copy(done.at[part], out_ref.at[part], sem.at[j])

    for j in range(slots // group):
        for n in range(j * group, (j + 1) * group):
            index = recv[0, n]
            k, r = split_by(index, CAP)
            p1 = rows[k, pl.ds(r, 1)]
            p2 = rows[k, pl.ds(r + CAP, 1)]
            done[n] = held[index] + m1 * p1 + m2 * p2
        write(j).start()
    for j in range(slots // group):
        write(j).wait()


def call(kernel, out_shape, in_specs, out_specs, args, scratch=(), aliases=None):
    return pl.pallas_call(
        kernel,
        out_shape=out_shape,
        in_specs=in_specs,
        out_specs=out_specs,
        scratch_shapes=scratch,
        input_output_aliases=aliases or {},
        compiler_params=pltpu.CompilerParams(vmem_limit_bytes=GRANT),
    )(*args)


def f32(*shape):
    return jax.ShapeDtypeStruct(shape, jnp.float32)


def i32(*shape):
    return jax.ShapeDtypeStruct(shape, jnp.int32)


def shifts(size):
    return [
        (i, i + 2 if i + 2 < size else i - 1) if i % 2 else (i, i - 2 if i >= 2 else i + 1)
        for i in range(size)
    ]


def swaps(size, odd):
    if not odd:
        return [(i, i ^ 1) for i in range(size)]
    return [(i, min(max(((i + 1) ^ 1) - 1, 0), size - 1)) for i in range(size)]


def distances(slabs):
    chips = slabs // 2
    early = range(chips // 2, chips - max(1, chips // 8))
    return [k for k in range(1, chips) if k not in early], list(early)


def shards(
    pressure, storage, trans, source, shells_old, shell_cap, shell_trans, new_source, cell_block
):
    slabs, cols = lax.axis_size("slab"), lax.axis_size("col")
    height, width = pressure.shape
    old_slots, count, cells = shells_old.shape[1:]
    new_slots = new_source.shape[1] // slabs
    chips = slabs // 2
    shells = shells_old[0]
    cap_row, trans_row = shell_cap.reshape(1, count), shell_trans.reshape(1, count)

    tall = height + 2 * EDGE
    tail = STEPS * CAP
    late_k, early_k = distances(slabs)

    def chip_swap(value, k):
        return lax.ppermute(value, "slab", [(i, i ^ (2 * k)) for i in range(slabs)])

    hopped = lax.ppermute(shells, "slab", swaps(slabs, False))
    plane, edge = f32(height, width), f32(FIELDS, EDGE, width)
    (
        inverse, const, slot, table, block_row, cap_row, trans_row, held,
        pressure, storage, trans, source, base1, base2, coef, edge_a, edge_b,
    ) = call(
        base_kernel,
        (
            f32(count, LANES), f32(1, LANES), i32(1, slabs * CAP), i32(*new_source.shape),
            i32(*cell_block.shape), f32(1, count), f32(1, count), f32(old_slots, count, cells),
            *(plane,) * 7, edge, edge,
        ),
        [HBM] * 9,
        (VMEM,) * 17,
        tuple(
            pltpu.with_memory_space_constraint(value, pltpu.HBM)
            for value in (
                cap_row, trans_row, new_source, cell_block, shells, pressure, storage, trans, source
            )
        ),
        [
            pltpu.VMEM((3, width // LANES, height, LANES), jnp.float32),
            pltpu.SMEM(cell_block.shape, jnp.int32),
            pltpu.SemaphoreType.DMA((9,)),
            pltpu.SemaphoreType.DMA((4,)),
        ],
    )
    edge_b = lax.ppermute(edge_b, "slab", shifts(slabs))
    edge_b = lax.ppermute(edge_b, "slab", swaps(slabs, False))
    edge_a = lax.ppermute(edge_a, "slab", swaps(slabs, False))
    packed = call(
        pack_kernel,
        tuple(f32(CAP, count + (tail if k in late_k else 0), cells) for k in range(chips)),
        [SMEM, VMEM, VMEM],
        (VMEM,) * chips,
        (slot, held, hopped),
    )
    side, place, recv = call(
        side_kernel,
        (f32(tall, LANES), i32(1, slabs * CAP), i32(1, new_slots)),
        [VMEM] * 11,
        (VMEM,) * 3,
        (
            table, block_row, pressure, storage, trans, source, base1, base2, coef,
            edge_a, edge_b,
        ),
    )
    side_c = lax.ppermute(side, "col", swaps(cols, False))
    side_d = lax.ppermute(side, "col", swaps(cols, True)) if cols > 2 else side_c
    blocks = {0: packed[0]}
    for k in early_k:
        blocks[k] = chip_swap(packed[k], k)

    result, rows = call(
        fracture_kernel,
        (plane, f32(slabs, tail, LANES)),
        [VMEM] * 13,
        (VMEM, VMEM),
        (
            place, const, pressure, storage, trans, source, base1, base2, coef,
            edge_a, edge_b, side_c, side_d,
        ),
        [
            pltpu.VMEM((STEPS, width // LANES, height, LANES), jnp.float32),
            pltpu.SMEM(place.shape, jnp.int32),
            pltpu.SemaphoreType.DMA,
        ],
    )
    other_rows = lax.ppermute(rows, "slab", swaps(slabs, False))
    local_rows, *filled = call(
        functools.partial(rows_kernel, late_k, early_k),
        (f32(tail, cells),)
        + (f32(CAP, count + tail, cells),) * len(late_k)
        + (f32(tail, cells),) * len(early_k),
        [VMEM] * (2 + len(late_k)),
        (VMEM,) * chips,
        (rows, other_rows, *(packed[k] for k in late_k)),
        aliases={2 + i: 1 + i for i in range(len(late_k))},
    )
    for k, value in zip(late_k, filled):
        blocks[k] = chip_swap(value, k)
    loose = [chip_swap(value, k) for k, value in zip(early_k, filled[len(late_k) :])]
    ready_k = [k for k in range(chips) if k not in late_k]
    left, coefficients, product = call(
        product_kernel,
        (
            jax.ShapeDtypeStruct((count, 3 * count), jnp.bfloat16),
            f32(2, count, LANES),
            f32(len(ready_k) * CAP, count, cells),
        ),
        [VMEM] * (3 + len(ready_k)),
        (VMEM,) * 3,
        (cap_row, trans_row, inverse, *(blocks[k] for k in ready_k)),
    )
    loose_k = [0, *early_k]
    shells_new = call(
        functools.partial(final_kernel, ready_k, late_k, loose_k),
        f32(new_slots, count, cells),
        [VMEM] * (4 + chips),
        ANY,
        (
            recv, left, coefficients, product,
            *(blocks[k] for k in late_k), local_rows, *loose,
        ),
        [
            pltpu.VMEM((chips * CAP, count, cells), jnp.float32),
            pltpu.VMEM((chips, tail, cells), jnp.float32),
            pltpu.VMEM((new_slots, count, cells), jnp.float32),
            pltpu.SMEM(recv.shape, jnp.int32),
            pltpu.SemaphoreType.DMA,
            pltpu.SemaphoreType.DMA((new_slots // 4,)),
        ],
    )
    return (result, shells_new[None])


def solution(mesh):
    placed_at = (
        P("slab", "col"),
        P("slab", "col"),
        P("slab", "col"),
        P("slab", "col"),
        P("col", "slab", None, None),
        P(),
        P(),
        P("col", None),
        P("col", "slab"),
    )
    return jax.shard_map(
        shards,
        mesh=mesh,
        in_specs=placed_at,
        out_specs=(P("slab", "col"), P("col", "slab", None, None)),
        check_vma=False,
    )
```

```python
import functools

import jax
import jax.numpy as jnp
from jax import lax
from jax.experimental import pallas as pl
from jax.experimental.pallas import tpu as pltpu
from jax.sharding import PartitionSpec as P


CAP = 4
STEPS = 2
ITERS = 3
EDGE = 8
LANES = 128
FIELDS = 7
GRANT = 16 * 2**20
FILL = (1.0, 1.0, 0.0, 0.0, 0.0, 0.0, 0.0)


VMEM = pl.BlockSpec(memory_space=pltpu.VMEM)
SMEM = pl.BlockSpec(memory_space=pltpu.SMEM)
ANY = pl.BlockSpec(memory_space=pl.ANY)
HBM = pl.BlockSpec(memory_space=pltpu.HBM)


def iota(shape, dim):
    return lax.broadcasted_iota(jnp.int32, shape, dim)


def split_by(value, size):
    if size & (size - 1) == 0:
        return value >> (size.bit_length() - 1), value & (size - 1)
    return value // size, value % size


def column_of(row, eye):
    return jnp.sum(jnp.where(eye, row, 0.0), axis=1, keepdims=True)


def row_of(column, count):
    eye = iota((count, count), 0) == iota((count, count), 1)
    return jnp.sum(jnp.where(eye, column, 0.0), axis=0, keepdims=True)


def placed(target, value, count):
    width = target.shape[1]
    hit = iota((count, width), 0) == target
    column = jnp.sum(jnp.where(hit, value.astype(jnp.float32), 0.0), axis=1, keepdims=True)
    return row_of(column, count).astype(jnp.int32)


def inverse_of(cap_row, trans_row):
    count = cap_row.shape[1]
    rows, cols = iota((count, count), 0), iota((count, count), 1)
    eye = rows == cols
    cap = column_of(cap_row, eye)
    trans = column_of(trans_row, eye)
    above = column_of(trans_row, cols == rows + 1)
    shape = (count, LANES)
    diag = jnp.broadcast_to(cap + trans + above, shape)
    low = jnp.broadcast_to(jnp.where(iota((count, 1), 0) == 0, 0.0, trans), shape)
    high = jnp.broadcast_to(above, shape)
    rhs = jnp.where(iota(shape, 0) == iota(shape, 1), 1.0, 0.0)
    step = 1
    while step < count:
        down = functools.partial(pltpu.roll, shift=step, axis=0)
        up = functools.partial(pltpu.roll, shift=count - step, axis=0)
        once = 1.0 / diag
        alpha = low * down(once)
        gamma = high * up(once)
        diag = diag - alpha * down(high) - gamma * up(low)
        rhs = rhs + alpha * down(rhs) + gamma * up(rhs)
        low, high = alpha * down(low), gamma * up(high)
        step *= 2
    return rhs / diag, cap


def sent_blocks(table, old_slots, slabs):
    me = lax.axis_index("slab")
    total = table.shape[1]
    new_slots = total // slabs
    anchor, local = split_by(table, old_slots)
    dest, within = split_by(iota((1, total), 1), new_slots)
    mine = anchor == me - me % 2
    seen = jnp.where(mine, 1, 0)
    shift = 1
    while shift < new_slots:
        seen = seen + jnp.where(within >= shift, pltpu.roll(seen, shift, axis=1), 0)
        shift *= 2
    return mine, dest, jnp.minimum(seen, CAP) - 1, local


def pack_sides(get, rows):
    lane = iota((rows, LANES), 1)
    out = jnp.zeros((rows, LANES), jnp.float32)
    for f in range(FIELDS):
        value = get(f)
        first, last = value[:, :LANES], value[:, -LANES:]
        at = 2 * EDGE * f
        moved = pltpu.roll(first, at, axis=1) if at else first
        out = jnp.where((lane >= at) & (lane < at + EDGE), moved, out)
        moved = pltpu.roll(last, (at + 2 * EDGE) % LANES, axis=1)
        out = jnp.where((lane >= at + EDGE) & (lane < at + 2 * EDGE), moved, out)
    return out


def base_kernel(
    cap_hbm, trans_hbm, table_hbm, block_hbm, shells_hbm, p_hbm, storage_hbm, t_hbm, source_hbm,
    inv_ref, const_ref, slot_ref, place_ref, recv_ref, cap_ref, trans_ref, held,
    p_ref, storage_ref, t_ref, source_ref, b1_ref, b2_ref, e_ref, a_ref, b_ref,
    tiles, table_ref, block_row, block_ref, sem, chunk_sem,
):
    me = lax.axis_index("slab")
    slabs = lax.axis_size("slab")
    even = me % 2 == 0
    old_slots, count, _ = shells_hbm.shape
    chunks = 4
    per = old_slots // chunks
    loads = [
        pltpu.make_async_copy(source, target, sem.at[i])
        for i, (source, target) in enumerate((
            (cap_hbm, cap_ref), (trans_hbm, trans_ref), (p_hbm, p_ref), (storage_hbm, storage_ref),
            (t_hbm, t_ref), (source_hbm, source_ref), (table_hbm, table_ref),
            (block_hbm, block_row), (block_hbm, block_ref),
        ))
    ]
    for load in loads:
        load.start()

    def chunk(i):
        part = pl.ds(i * per, per)
        return pltpu.make_async_copy(shells_hbm.at[part], held.at[part], chunk_sem.at[i])

    @pl.when(even)
    def _():
        for i in range(chunks):
            chunk(i).start()

    for load in loads:
        load.wait()
    cap_row, trans_row = cap_ref[...], trans_ref[...]
    inverse, cap = inverse_of(cap_row, trans_row)
    inv_ref[...] = inverse
    t0 = trans_row[:, 0:1]
    first_row = inverse[0:1, :count] * cap_row
    w1 = inverse[:, 0:1] * cap
    w2 = cap * jnp.sum(inverse[:, :count] * first_row, axis=1, keepdims=True)
    couple_row = inverse[0:1, :count] * t0
    c0 = couple_row[:, 0:1]
    c1 = jnp.sum(first_row * couple_row, axis=1, keepdims=True)
    coupling = t0 * (1.0 - c0)
    const_ref[...] = jnp.broadcast_to(t0 * c1 / coupling, const_ref.shape)

    tiles[...] = jnp.zeros_like(tiles)

    @pl.when(even)
    def _():
        v1 = jnp.broadcast_to(t0 * w1, (count, LANES))
        v2 = jnp.broadcast_to(t0 * w2, (count, LANES))
        on = jnp.broadcast_to(coupling, (1, LANES))
        per_row = p_ref.shape[1] // LANES
        for i in range(chunks):
            chunk(i).wait()

            for slot in range(i * per, (i + 1) * per):
                data = held[slot]
                row, half = split_by(block_ref[0, slot], per_row)
                at = pl.ds(row, 1)
                tiles[0, half, at] = jnp.sum(v1 * data, axis=0, keepdims=True)
                tiles[1, half, at] = jnp.sum(v2 * data, axis=0, keepdims=True)
                tiles[2, half, at] = on

    for i, ref in enumerate((b1_ref, b2_ref, e_ref)):
        ref[...] = jnp.concatenate([tiles[i, h] for h in range(tiles.shape[1])], axis=1)
    fields = (p_ref, storage_ref, t_ref, source_ref, b1_ref, b2_ref, e_ref)
    height = p_ref.shape[0]
    for f, ref in enumerate(fields):
        top, bottom = ref[0:EDGE, :], ref[height - EDGE : height, :]
        a_ref[f] = jnp.where(even, bottom, top)
        b_ref[f] = jnp.where(even, top, bottom)
    table = table_ref[...]
    total = table.shape[1]
    mine, dest, rank, local = sent_blocks(table, old_slots, slabs)
    distance = (dest >> 1) ^ (me // 2)
    here = mine & ((dest & 1) == me % 2)
    slot_ref[...] = placed(jnp.where(here, distance * CAP + rank, -1), local, slot_ref.shape[1])
    eye = iota((old_slots, old_slots), 0) == iota((old_slots, old_slots), 1)
    column = column_of(block_row[...].astype(jnp.float32), eye)
    owner = iota((old_slots, total), 0) == local
    block = jnp.sum(jnp.where(owner, column, 0.0), axis=0, keepdims=True)
    place_ref[...] = placed(jnp.where(mine, dest * CAP + rank, -1), block, slabs * CAP)

    count = recv_ref.shape[1]
    anchor, _ = split_by(placed(iota((1, total), 1) - me * count, table, count), old_slots)
    row, above = iota((count, count), 0), iota((count, count), 1)
    column = column_of(anchor.astype(jnp.float32), row == above)
    same = (column == anchor.astype(jnp.float32)) & (above < row)
    rank = row_of(jnp.sum(jnp.where(same, 1.0, 0.0), axis=1, keepdims=True), count)
    rank = jnp.minimum(rank.astype(jnp.int32), CAP - 1)
    recv_ref[...] = ((anchor >> 1) ^ (me // 2)) * CAP + rank


def pack_kernel(slot_ref, own_ref, other_ref, *out_refs):
    core = lax.axis_index("slab") % 2
    count = own_ref.shape[1]

    def fill(source):
        for k, ref in enumerate(out_refs):
            for r in range(CAP):
                ref[r, :count] = source[slot_ref[0, k * CAP + r]]

    @pl.when(core == 0)
    def _():
        fill(own_ref)

    @pl.when(core == 1)
    def _():
        fill(other_ref)


def rows_kernel(late_k, early_k, own_ref, other_ref, *rest):
    local_ref, *outs = rest[len(late_k) :]
    me = lax.axis_index("slab")

    def rows(k):
        at = ((me // 2) ^ k) * 2 + me % 2
        return jnp.where(me % 2 == 0, own_ref[at], other_ref[at])

    local_ref[...] = rows(0)
    for k, ref in zip(late_k, outs):
        value = rows(k)
        ref[0, ref.shape[1] - value.shape[0] :] = value
    for k, ref in zip(early_k, outs[len(late_k) :]):
        ref[...] = rows(k)


def side_kernel(*refs):
    *fields, a_ref, b_ref, out_ref = refs
    even = lax.axis_index("slab") % 2 == 0
    height = fields[0].shape[0]
    from_a = pack_sides(lambda f: a_ref[f], EDGE)
    from_b = pack_sides(lambda f: b_ref[f], EDGE)
    out_ref[0:EDGE] = jnp.where(even, from_b, from_a)
    out_ref[EDGE : EDGE + height] = pack_sides(lambda f: fields[f][...], height)
    out_ref[EDGE + height :] = jnp.where(even, from_a, from_b)


def fracture_kernel(
    place_ref, const_ref, p_ref, storage_ref, t_ref, source_ref, b1_ref, b2_ref, e_ref,
    a_ref, b_ref, c_ref, d_ref, out_ref, rows_ref, keep, place, sem,
):
    table = pltpu.make_async_copy(place_ref, place, sem)
    table.start()
    me, slabs = lax.axis_index("slab"), lax.axis_size("slab")
    col, cols = lax.axis_index("col"), lax.axis_size("col")
    even, col_even = me % 2 == 0, col % 2 == 0
    height, width = p_ref.shape
    tall, wide = height + 2 * EDGE, width + LANES
    row, lane = iota((tall, wide), 0), iota((tall, wide), 1)
    missing = (
        ((me == 0) & (row < EDGE))
        | ((me == slabs - 1) & (row >= EDGE + height))
        | ((lane >= width) & (lane < wide - EDGE) & ((lane >= width + EDGE) | (col == cols - 1)))
        | ((lane >= wide - EDGE) & (col == 0))
    )
    side_lane = iota((tall, LANES), 1)
    right = jnp.where(col_even, c_ref[...], d_ref[...])
    left = jnp.where(col_even, d_ref[...], c_ref[...])
    refs = (p_ref, storage_ref, t_ref, source_ref, b1_ref, b2_ref, e_ref)

    def extended(f):
        top = jnp.where(even, b_ref[f], a_ref[f])
        bottom = jnp.where(even, a_ref[f], b_ref[f])
        own = jnp.concatenate([top, refs[f][...], bottom], axis=0)
        at = 2 * EDGE * f
        from_right = pltpu.roll(right, LANES - at, axis=1) if at else right
        from_left = pltpu.roll(left, LANES - 2 * EDGE - at, axis=1)
        side = jnp.where(side_lane < EDGE, from_right, from_left)
        return jnp.where(missing, FILL[f], jnp.concatenate([own, side], axis=1))

    p, storage, t, source, base1, base2, coef = (extended(f) for f in range(FIELDS))
    next_lane = functools.partial(pltpu.roll, shift=wide - 1, axis=1)
    prev_lane = functools.partial(pltpu.roll, shift=1, axis=1)
    next_row = functools.partial(pltpu.roll, shift=tall - 1, axis=0)
    prev_row = functools.partial(pltpu.roll, shift=1, axis=0)

    def face_of(near):
        total = t + near
        return jnp.where(total > 0.0, 2.0 * t * near / jnp.where(total > 0.0, total, 1.0), 0.0)

    face_h, face_v = face_of(next_lane(t)), face_of(next_row(t))
    conduct = face_h + prev_lane(face_h) + face_v + prev_row(face_v)
    half_h, half_v = face_h * 0.5, face_v * 0.5
    fixed = storage + coef
    rhs = source + base1
    ratio = const_ref[0:1, 0:1]
    for step in range(STEPS):
        prev = p
        for sweep in range(ITERS):
            if sweep == ITERS - 1:
                mid = p[EDGE : EDGE + height]
                for h in range(width // LANES):
                    keep[step, h] = mid[:, h * LANES : (h + 1) * LANES]
                last = p
            square = p * p
            if step == STEPS - 1 and sweep == ITERS - 1:
                break
            flow_h = half_h * (next_lane(square) - square)
            flow_v = half_v * (next_row(square) - square)
            flux = flow_h - prev_lane(flow_h) + flow_v - prev_row(flow_v)
            misfit = storage * (p - prev) - flux + coef * p - rhs
            p = p - misfit / (fixed + p * conduct)
        if step < STEPS - 1:
            rhs = source + base2 + ratio * coef * last

    def own(value):
        return value[EDGE : EDGE + height, :width]

    strip, slab = square[EDGE : EDGE + height], square[:, :width]
    flow_h = half_h[EDGE : EDGE + height] * (next_lane(strip) - strip)
    flow_v = half_v[:, :width] * (next_row(slab) - slab)
    flux = (flow_h - prev_lane(flow_h))[:, :width] + (flow_v - prev_row(flow_v))[EDGE : EDGE + height]
    p, prev = own(p), own(prev)
    misfit = own(storage) * (p - prev) - flux + own(coef) * p - own(rhs)
    out_ref[...] = p - misfit / (own(fixed) + p * own(conduct))

    table.wait()
    for q in range(rows_ref.shape[0] * CAP):
        d, r = q // CAP, q % CAP
        at_row, half = split_by(place[0, q], width // LANES)
        for step in range(STEPS):
            rows_ref[d, pl.ds(step * CAP + r, 1)] = keep[step, half, pl.ds(at_row, 1)]


def multiply(left, blocks):
    results = []
    for first in range(0, len(blocks), 2):
        parts = []
        for data in blocks[first : first + 2]:
            hi = data.astype(jnp.bfloat16)
            lo = (data - hi.astype(jnp.float32)).astype(jnp.bfloat16)
            parts.append(jnp.concatenate([hi, lo, hi], axis=0))
        product = jnp.dot(left, jnp.concatenate(parts, axis=1), preferred_element_type=jnp.float32)
        results += [product[:, :LANES], product[:, LANES:]]
    return results


def product_kernel(cap_ref, trans_ref, inv_ref, *rest):
    *blocks, left_ref, m_ref, out_ref = rest
    count = cap_ref.shape[1]
    inverse = inv_ref[:, :count]
    t0 = trans_ref[:, 0:1]
    a = inverse * cap_ref[...]
    couple = inv_ref[:, 0:1] * t0
    couple2 = jnp.sum(a * (inverse[0:1, :] * t0), axis=1, keepdims=True)
    square = jnp.dot(a, a, preferred_element_type=jnp.float32, precision=lax.Precision.HIGHEST)
    high = square.astype(jnp.bfloat16)
    low = (square - high.astype(jnp.float32)).astype(jnp.bfloat16)
    left = jnp.concatenate([high, high, low], axis=1)
    left_ref[...] = left
    m_ref[0] = jnp.broadcast_to(couple2, (count, LANES))
    m_ref[1] = jnp.broadcast_to(couple, (count, LANES))
    for i, ref in enumerate(blocks):
        for r, value in enumerate(multiply(left, [ref[r, :count] for r in range(CAP)])):
            out_ref[i * CAP + r] = value


def final_kernel(ready_k, tailed_k, loose_k, recv_ref, left_ref, m_ref, product_ref, *rest):
    *in_refs, out_ref, held, rows, done, recv, recv_sem, sem = rest
    slots, count = out_ref.shape[:2]
    table = pltpu.make_async_copy(recv_ref, recv, recv_sem)
    table.start()
    for i, k in enumerate(ready_k):
        held[pl.ds(k * CAP, CAP)] = product_ref[pl.ds(i * CAP, CAP)]
    left = left_ref[...]
    for k, ref in zip(tailed_k, in_refs):
        rows[k] = ref[0, count:]
        if k not in ready_k:
            for r, value in enumerate(multiply(left, [ref[r, :count] for r in range(CAP)])):
                held[k * CAP + r] = value
    for k, ref in zip(loose_k, in_refs[len(tailed_k) :]):
        rows[k] = ref[...]
    m1, m2 = m_ref[0], m_ref[1]
    group = 4
    table.wait()

    def write(j):
        part = pl.ds(j * group, group)
        return pltpu.make_async_copy(done.at[part], out_ref.at[part], sem.at[j])

    for j in range(slots // group):
        for n in range(j * group, (j + 1) * group):
            index = recv[0, n]
            k, r = split_by(index, CAP)
            p1 = rows[k, pl.ds(r, 1)]
            p2 = rows[k, pl.ds(r + CAP, 1)]
            done[n] = held[index] + m1 * p1 + m2 * p2
        write(j).start()
    for j in range(slots // group):
        write(j).wait()


def call(kernel, out_shape, in_specs, out_specs, args, scratch=(), aliases=None):
    return pl.pallas_call(
        kernel,
        out_shape=out_shape,
        in_specs=in_specs,
        out_specs=out_specs,
        scratch_shapes=scratch,
        input_output_aliases=aliases or {},
        compiler_params=pltpu.CompilerParams(vmem_limit_bytes=GRANT),
    )(*args)


def f32(*shape):
    return jax.ShapeDtypeStruct(shape, jnp.float32)


def i32(*shape):
    return jax.ShapeDtypeStruct(shape, jnp.int32)


def shifts(size):
    return [
        (i, i + 2 if i + 2 < size else i - 1) if i % 2 else (i, i - 2 if i >= 2 else i + 1)
        for i in range(size)
    ]


def swaps(size, odd):
    if not odd:
        return [(i, i ^ 1) for i in range(size)]
    return [(i, min(max(((i + 1) ^ 1) - 1, 0), size - 1)) for i in range(size)]


def distances(slabs):
    chips = slabs // 2
    early = range(chips // 2, chips - max(1, chips // 8))
    return [k for k in range(1, chips) if k not in early], list(early)


def shards(
    pressure, storage, trans, source, shells_old, shell_cap, shell_trans, new_source, cell_block
):
    slabs, cols = lax.axis_size("slab"), lax.axis_size("col")
    height, width = pressure.shape
    old_slots, count, cells = shells_old.shape[1:]
    new_slots = new_source.shape[1] // slabs
    chips = slabs // 2
    shells = shells_old[0]
    cap_row, trans_row = shell_cap.reshape(1, count), shell_trans.reshape(1, count)

    tall = height + 2 * EDGE
    tail = STEPS * CAP
    late_k, early_k = distances(slabs)

    def chip_swap(value, k):
        return lax.ppermute(value, "slab", [(i, i ^ (2 * k)) for i in range(slabs)])

    hopped = lax.ppermute(shells, "slab", swaps(slabs, False))
    plane, edge = f32(height, width), f32(FIELDS, EDGE, width)
    (
        inverse, const, slot, place, recv, cap_row, trans_row, held,
        pressure, storage, trans, source, base1, base2, coef, edge_a, edge_b,
    ) = call(
        base_kernel,
        (
            f32(count, LANES), f32(1, LANES), i32(1, chips * CAP), i32(1, slabs * CAP),
            i32(1, new_slots), f32(1, count), f32(1, count), f32(old_slots, count, cells),
            *(plane,) * 7, edge, edge,
        ),
        [HBM] * 9,
        (VMEM,) * 17,
        tuple(
            pltpu.with_memory_space_constraint(value, pltpu.HBM)
            for value in (
                cap_row, trans_row, new_source, cell_block, shells, pressure, storage, trans, source
            )
        ),
        [
            pltpu.VMEM((3, width // LANES, height, LANES), jnp.float32),
            pltpu.VMEM(new_source.shape, jnp.int32),
            pltpu.VMEM(cell_block.shape, jnp.int32),
            pltpu.SMEM(cell_block.shape, jnp.int32),
            pltpu.SemaphoreType.DMA((9,)),
            pltpu.SemaphoreType.DMA((4,)),
        ],
    )
    edge_b = lax.ppermute(edge_b, "slab", shifts(slabs))
    edge_b = lax.ppermute(edge_b, "slab", swaps(slabs, False))
    edge_a = lax.ppermute(edge_a, "slab", swaps(slabs, False))
    packed = call(
        pack_kernel,
        tuple(f32(CAP, count + (tail if k in late_k else 0), cells) for k in range(chips)),
        [VMEM, VMEM, VMEM],
        (VMEM,) * chips,
        (slot, held, hopped),
    )
    side = call(
        side_kernel,
        f32(tall, LANES),
        [VMEM] * 9,
        VMEM,
        (pressure, storage, trans, source, base1, base2, coef, edge_a, edge_b),
    )
    side_c = lax.ppermute(side, "col", swaps(cols, False))
    side_d = lax.ppermute(side, "col", swaps(cols, True)) if cols > 2 else side_c
    blocks = {0: packed[0]}
    for k in early_k:
        blocks[k] = chip_swap(packed[k], k)

    result, rows = call(
        fracture_kernel,
        (plane, f32(slabs, tail, LANES)),
        [VMEM] * 13,
        (VMEM, VMEM),
        (
            place, const, pressure, storage, trans, source, base1, base2, coef,
            edge_a, edge_b, side_c, side_d,
        ),
        [
            pltpu.VMEM((STEPS, width // LANES, height, LANES), jnp.float32),
            pltpu.SMEM(place.shape, jnp.int32),
            pltpu.SemaphoreType.DMA,
        ],
    )
    other_rows = lax.ppermute(rows, "slab", swaps(slabs, False))
    local_rows, *filled = call(
        functools.partial(rows_kernel, late_k, early_k),
        (f32(tail, cells),)
        + (f32(CAP, count + tail, cells),) * len(late_k)
        + (f32(tail, cells),) * len(early_k),
        [VMEM] * (2 + len(late_k)),
        (VMEM,) * chips,
        (rows, other_rows, *(packed[k] for k in late_k)),
        aliases={2 + i: 1 + i for i in range(len(late_k))},
    )
    for k, value in zip(late_k, filled):
        blocks[k] = chip_swap(value, k)
    loose = [chip_swap(value, k) for k, value in zip(early_k, filled[len(late_k) :])]
    ready_k = [k for k in range(chips) if k not in late_k]
    left, coefficients, product = call(
        product_kernel,
        (
            jax.ShapeDtypeStruct((count, 3 * count), jnp.bfloat16),
            f32(2, count, LANES),
            f32(len(ready_k) * CAP, count, cells),
        ),
        [VMEM] * (3 + len(ready_k)),
        (VMEM,) * 3,
        (cap_row, trans_row, inverse, *(blocks[k] for k in ready_k)),
    )
    loose_k = [0, *early_k]
    shells_new = call(
        functools.partial(final_kernel, ready_k, late_k, loose_k),
        f32(new_slots, count, cells),
        [VMEM] * (4 + chips),
        ANY,
        (
            recv, left, coefficients, product,
            *(blocks[k] for k in late_k), local_rows, *loose,
        ),
        [
            pltpu.VMEM((chips * CAP, count, cells), jnp.float32),
            pltpu.VMEM((chips, tail, cells), jnp.float32),
            pltpu.VMEM((new_slots, count, cells), jnp.float32),
            pltpu.SMEM(recv.shape, jnp.int32),
            pltpu.SemaphoreType.DMA,
            pltpu.SemaphoreType.DMA((new_slots // 4,)),
        ],
    )
    return (result, shells_new[None])


def solution(mesh):
    placed_at = (
        P("slab", "col"),
        P("slab", "col"),
        P("slab", "col"),
        P("slab", "col"),
        P("col", "slab", None, None),
        P(),
        P(),
        P("col", None),
        P("col", "slab"),
    )
    return jax.shard_map(
        shards,
        mesh=mesh,
        in_specs=placed_at,
        out_specs=(P("slab", "col"), P("col", "slab", None, None)),
        check_vma=False,
    )
```

```python
import functools

import jax
import jax.numpy as jnp
from jax import lax
from jax.experimental import pallas as pl
from jax.experimental.pallas import tpu as pltpu
from jax.sharding import PartitionSpec as P


CAP = 4
STEPS = 2
ITERS = 3
EDGE = 8
LANES = 128
FIELDS = 7
GRANT = 16 * 2**20
FILL = (1.0, 1.0, 0.0, 0.0, 0.0, 0.0, 0.0)


VMEM = pl.BlockSpec(memory_space=pltpu.VMEM)
SMEM = pl.BlockSpec(memory_space=pltpu.SMEM)
ANY = pl.BlockSpec(memory_space=pl.ANY)
HBM = pl.BlockSpec(memory_space=pltpu.HBM)


def iota(shape, dim):
    return lax.broadcasted_iota(jnp.int32, shape, dim)


def split_by(value, size):
    if size & (size - 1) == 0:
        return value >> (size.bit_length() - 1), value & (size - 1)
    return value // size, value % size


def column_of(row, eye):
    return jnp.sum(jnp.where(eye, row, 0.0), axis=1, keepdims=True)


def row_of(column, count):
    eye = iota((count, count), 0) == iota((count, count), 1)
    return jnp.sum(jnp.where(eye, column, 0.0), axis=0, keepdims=True)


def placed(target, value, count):
    width = target.shape[1]
    hit = iota((count, width), 0) == target
    column = jnp.sum(jnp.where(hit, value.astype(jnp.float32), 0.0), axis=1, keepdims=True)
    return row_of(column, count).astype(jnp.int32)


def inverse_of(cap_row, trans_row):
    count = cap_row.shape[1]
    rows, cols = iota((count, count), 0), iota((count, count), 1)
    eye = rows == cols
    cap = column_of(cap_row, eye)
    trans = column_of(trans_row, eye)
    above = column_of(trans_row, cols == rows + 1)
    shape = (count, LANES)
    diag = jnp.broadcast_to(cap + trans + above, shape)
    low = jnp.broadcast_to(jnp.where(iota((count, 1), 0) == 0, 0.0, trans), shape)
    high = jnp.broadcast_to(above, shape)
    rhs = jnp.where(iota(shape, 0) == iota(shape, 1), 1.0, 0.0)
    step = 1
    while step < count:
        down = functools.partial(pltpu.roll, shift=step, axis=0)
        up = functools.partial(pltpu.roll, shift=count - step, axis=0)
        once = 1.0 / diag
        alpha = low * down(once)
        gamma = high * up(once)
        diag = diag - alpha * down(high) - gamma * up(low)
        rhs = rhs + alpha * down(rhs) + gamma * up(rhs)
        low, high = alpha * down(low), gamma * up(high)
        step *= 2
    return rhs / diag, cap


def sent_blocks(table, old_slots, slabs):
    me = lax.axis_index("slab")
    total = table.shape[1]
    new_slots = total // slabs
    anchor, local = split_by(table, old_slots)
    dest, within = split_by(iota((1, total), 1), new_slots)
    mine = anchor == me - me % 2
    seen = jnp.where(mine, 1, 0)
    shift = 1
    while shift < new_slots:
        seen = seen + jnp.where(within >= shift, pltpu.roll(seen, shift, axis=1), 0)
        shift *= 2
    return mine, dest, jnp.minimum(seen, CAP) - 1, local


def pack_sides(get, rows):
    lane = iota((rows, LANES), 1)
    out = jnp.zeros((rows, LANES), jnp.float32)
    for f in range(FIELDS):
        value = get(f)
        first, last = value[:, :LANES], value[:, -LANES:]
        at = 2 * EDGE * f
        moved = pltpu.roll(first, at, axis=1) if at else first
        out = jnp.where((lane >= at) & (lane < at + EDGE), moved, out)
        moved = pltpu.roll(last, (at + 2 * EDGE) % LANES, axis=1)
        out = jnp.where((lane >= at + EDGE) & (lane < at + 2 * EDGE), moved, out)
    return out


def base_kernel(
    cap_hbm, trans_hbm, table_hbm, block_hbm, shells_hbm, p_hbm, storage_hbm, t_hbm, source_hbm,
    inv_ref, const_ref, slot_ref, place_ref, recv_ref, cap_ref, trans_ref, held,
    p_ref, storage_ref, t_ref, source_ref, b1_ref, b2_ref, e_ref, a_ref, b_ref,
    tiles, table_ref, block_row, block_ref, sem, chunk_sem,
):
    me = lax.axis_index("slab")
    slabs = lax.axis_size("slab")
    even = me % 2 == 0
    old_slots, count, _ = shells_hbm.shape
    chunks = 4
    per = old_slots // chunks
    loads = [
        pltpu.make_async_copy(source, target, sem.at[i])
        for i, (source, target) in enumerate((
            (cap_hbm, cap_ref), (trans_hbm, trans_ref), (p_hbm, p_ref), (storage_hbm, storage_ref),
            (t_hbm, t_ref), (source_hbm, source_ref), (table_hbm, table_ref),
            (block_hbm, block_row), (block_hbm, block_ref),
        ))
    ]
    for load in loads:
        load.start()

    def chunk(i):
        part = pl.ds(i * per, per)
        return pltpu.make_async_copy(shells_hbm.at[part], held.at[part], chunk_sem.at[i])

    @pl.when(even)
    def _():
        for i in range(chunks):
            chunk(i).start()

    for load in loads[:2]:
        load.wait()
    cap_row, trans_row = cap_ref[...], trans_ref[...]
    inverse, cap = inverse_of(cap_row, trans_row)
    inv_ref[...] = inverse
    t0 = trans_row[:, 0:1]
    first_row = inverse[0:1, :count] * cap_row
    w1 = inverse[:, 0:1] * cap
    w2 = cap * jnp.sum(inverse[:, :count] * first_row, axis=1, keepdims=True)
    couple_row = inverse[0:1, :count] * t0
    c0 = couple_row[:, 0:1]
    c1 = jnp.sum(first_row * couple_row, axis=1, keepdims=True)
    coupling = t0 * (1.0 - c0)
    const_ref[...] = jnp.broadcast_to(t0 * c1 / coupling, const_ref.shape)

    for load in loads[2:]:
        load.wait()
    tiles[...] = jnp.zeros_like(tiles)

    @pl.when(even)
    def _():
        v1 = jnp.broadcast_to(t0 * w1, (count, LANES))
        v2 = jnp.broadcast_to(t0 * w2, (count, LANES))
        on = jnp.broadcast_to(coupling, (1, LANES))
        per_row = p_ref.shape[1] // LANES
        for i in range(chunks):
            chunk(i).wait()

            for slot in range(i * per, (i + 1) * per):
                data = held[slot]
                row, half = split_by(block_ref[0, slot], per_row)
                at = pl.ds(row, 1)
                tiles[0, half, at] = jnp.sum(v1 * data, axis=0, keepdims=True)
                tiles[1, half, at] = jnp.sum(v2 * data, axis=0, keepdims=True)
                tiles[2, half, at] = on

    for i, ref in enumerate((b1_ref, b2_ref, e_ref)):
        ref[...] = jnp.concatenate([tiles[i, h] for h in range(tiles.shape[1])], axis=1)
    fields = (p_ref, storage_ref, t_ref, source_ref, b1_ref, b2_ref, e_ref)
    height = p_ref.shape[0]
    for f, ref in enumerate(fields):
        top, bottom = ref[0:EDGE, :], ref[height - EDGE : height, :]
        a_ref[f] = jnp.where(even, bottom, top)
        b_ref[f] = jnp.where(even, top, bottom)
    table = table_ref[...]
    total = table.shape[1]
    mine, dest, rank, local = sent_blocks(table, old_slots, slabs)
    distance = (dest >> 1) ^ (me // 2)
    here = mine & ((dest & 1) == me % 2)
    slot_ref[...] = placed(jnp.where(here, distance * CAP + rank, -1), local, slot_ref.shape[1])
    eye = iota((old_slots, old_slots), 0) == iota((old_slots, old_slots), 1)
    column = column_of(block_row[...].astype(jnp.float32), eye)
    owner = iota((old_slots, total), 0) == local
    block = jnp.sum(jnp.where(owner, column, 0.0), axis=0, keepdims=True)
    place_ref[...] = placed(jnp.where(mine, dest * CAP + rank, -1), block, slabs * CAP)

    count = recv_ref.shape[1]
    anchor, _ = split_by(placed(iota((1, total), 1) - me * count, table, count), old_slots)
    row, above = iota((count, count), 0), iota((count, count), 1)
    column = column_of(anchor.astype(jnp.float32), row == above)
    same = (column == anchor.astype(jnp.float32)) & (above < row)
    rank = row_of(jnp.sum(jnp.where(same, 1.0, 0.0), axis=1, keepdims=True), count)
    rank = jnp.minimum(rank.astype(jnp.int32), CAP - 1)
    recv_ref[...] = ((anchor >> 1) ^ (me // 2)) * CAP + rank


def pack_kernel(slot_ref, own_ref, other_ref, *out_refs):
    core = lax.axis_index("slab") % 2
    count = own_ref.shape[1]

    def fill(source):
        for k, ref in enumerate(out_refs):
            for r in range(CAP):
                ref[r * count : (r + 1) * count] = source[slot_ref[0, k * CAP + r]]

    @pl.when(core == 0)
    def _():
        fill(own_ref)

    @pl.when(core == 1)
    def _():
        fill(other_ref)


def rows_kernel(late_k, early_k, own_ref, other_ref, *rest):
    local_ref, *outs = rest[len(late_k) :]
    me = lax.axis_index("slab")

    def rows(k):
        at = ((me // 2) ^ k) * 2 + me % 2
        return jnp.where(me % 2 == 0, own_ref[at], other_ref[at])

    local_ref[...] = rows(0)
    for k, ref in zip(late_k, outs):
        value = rows(k)
        ref[ref.shape[0] - value.shape[0] :] = value
    for k, ref in zip(early_k, outs[len(late_k) :]):
        ref[...] = rows(k)


def side_kernel(*refs):
    *fields, a_ref, b_ref, out_ref = refs
    even = lax.axis_index("slab") % 2 == 0
    height = fields[0].shape[0]
    from_a = pack_sides(lambda f: a_ref[f], EDGE)
    from_b = pack_sides(lambda f: b_ref[f], EDGE)
    out_ref[0:EDGE] = jnp.where(even, from_b, from_a)
    out_ref[EDGE : EDGE + height] = pack_sides(lambda f: fields[f][...], height)
    out_ref[EDGE + height :] = jnp.where(even, from_a, from_b)


def fracture_kernel(
    place_ref, const_ref, p_ref, storage_ref, t_ref, source_ref, b1_ref, b2_ref, e_ref,
    a_ref, b_ref, c_ref, d_ref, out_ref, rows_ref, keep, place, sem,
):
    table = pltpu.make_async_copy(place_ref, place, sem)
    table.start()
    me, slabs = lax.axis_index("slab"), lax.axis_size("slab")
    col, cols = lax.axis_index("col"), lax.axis_size("col")
    even, col_even = me % 2 == 0, col % 2 == 0
    height, width = p_ref.shape
    tall, wide = height + 2 * EDGE, width + LANES
    row, lane = iota((tall, wide), 0), iota((tall, wide), 1)
    missing = (
        ((me == 0) & (row < EDGE))
        | ((me == slabs - 1) & (row >= EDGE + height))
        | ((lane >= width) & (lane < wide - EDGE) & ((lane >= width + EDGE) | (col == cols - 1)))
        | ((lane >= wide - EDGE) & (col == 0))
    )
    side_lane = iota((tall, LANES), 1)
    right = jnp.where(col_even, c_ref[...], d_ref[...])
    left = jnp.where(col_even, d_ref[...], c_ref[...])
    refs = (p_ref, storage_ref, t_ref, source_ref, b1_ref, b2_ref, e_ref)

    def extended(f):
        top = jnp.where(even, b_ref[f], a_ref[f])
        bottom = jnp.where(even, a_ref[f], b_ref[f])
        own = jnp.concatenate([top, refs[f][...], bottom], axis=0)
        at = 2 * EDGE * f
        from_right = pltpu.roll(right, LANES - at, axis=1) if at else right
        from_left = pltpu.roll(left, LANES - 2 * EDGE - at, axis=1)
        side = jnp.where(side_lane < EDGE, from_right, from_left)
        return jnp.where(missing, FILL[f], jnp.concatenate([own, side], axis=1))

    p, storage, t, source, base1, base2, coef = (extended(f) for f in range(FIELDS))
    next_lane = functools.partial(pltpu.roll, shift=wide - 1, axis=1)
    prev_lane = functools.partial(pltpu.roll, shift=1, axis=1)
    next_row = functools.partial(pltpu.roll, shift=tall - 1, axis=0)
    prev_row = functools.partial(pltpu.roll, shift=1, axis=0)

    def face_of(near):
        total = t + near
        return jnp.where(total > 0.0, 2.0 * t * near / jnp.where(total > 0.0, total, 1.0), 0.0)

    face_h, face_v = face_of(next_lane(t)), face_of(next_row(t))
    conduct = face_h + prev_lane(face_h) + face_v + prev_row(face_v)
    half_h, half_v = face_h * 0.5, face_v * 0.5
    fixed = storage + coef
    rhs = source + base1
    ratio = const_ref[0:1, 0:1]
    for step in range(STEPS):
        prev = p
        for sweep in range(ITERS):
            if sweep == ITERS - 1:
                mid = p[EDGE : EDGE + height]
                for h in range(width // LANES):
                    keep[step, h] = mid[:, h * LANES : (h + 1) * LANES]
                last = p
            square = p * p
            if step == STEPS - 1 and sweep == ITERS - 1:
                break
            flow_h = half_h * (next_lane(square) - square)
            flow_v = half_v * (next_row(square) - square)
            flux = flow_h - prev_lane(flow_h) + flow_v - prev_row(flow_v)
            misfit = storage * (p - prev) - flux + coef * p - rhs
            p = p - misfit / (fixed + p * conduct)
        if step < STEPS - 1:
            rhs = source + base2 + ratio * coef * last

    def own(value):
        return value[EDGE : EDGE + height, :width]

    strip, slab = square[EDGE : EDGE + height], square[:, :width]
    flow_h = half_h[EDGE : EDGE + height] * (next_lane(strip) - strip)
    flow_v = half_v[:, :width] * (next_row(slab) - slab)
    flux = (flow_h - prev_lane(flow_h))[:, :width] + (flow_v - prev_row(flow_v))[EDGE : EDGE + height]
    p, prev = own(p), own(prev)
    misfit = own(storage) * (p - prev) - flux + own(coef) * p - own(rhs)
    out_ref[...] = p - misfit / (own(fixed) + p * own(conduct))

    table.wait()
    for q in range(rows_ref.shape[0] * CAP):
        d, r = q // CAP, q % CAP
        at_row, half = split_by(place[0, q], width // LANES)
        for step in range(STEPS):
            rows_ref[d, pl.ds(step * CAP + r, 1)] = keep[step, half, pl.ds(at_row, 1)]


def multiply(left, blocks):
    results = []
    for first in range(0, len(blocks), 2):
        parts = []
        for data in blocks[first : first + 2]:
            hi = data.astype(jnp.bfloat16)
            lo = (data - hi.astype(jnp.float32)).astype(jnp.bfloat16)
            parts.append(jnp.concatenate([hi, lo, hi], axis=0))
        product = jnp.dot(left, jnp.concatenate(parts, axis=1), preferred_element_type=jnp.float32)
        results += [product[:, :LANES], product[:, LANES:]]
    return results


def parts_of(ref, count):
    return [ref[r * count : (r + 1) * count] for r in range(CAP)]


def product_kernel(cap_ref, trans_ref, inv_ref, *rest):
    *blocks, left_ref, m_ref, out_ref = rest
    count = cap_ref.shape[1]
    inverse = inv_ref[:, :count]
    t0 = trans_ref[:, 0:1]
    a = inverse * cap_ref[...]
    couple = inv_ref[:, 0:1] * t0
    couple2 = jnp.sum(a * (inverse[0:1, :] * t0), axis=1, keepdims=True)
    square = jnp.dot(a, a, preferred_element_type=jnp.float32, precision=lax.Precision.HIGHEST)
    high = square.astype(jnp.bfloat16)
    low = (square - high.astype(jnp.float32)).astype(jnp.bfloat16)
    left = jnp.concatenate([high, high, low], axis=1)
    left_ref[...] = left
    m_ref[0] = jnp.broadcast_to(couple2, (count, LANES))
    m_ref[1] = jnp.broadcast_to(couple, (count, LANES))
    for i, ref in enumerate(blocks):
        for r, value in enumerate(multiply(left, parts_of(ref, count))):
            out_ref[i * CAP + r] = value


def final_kernel(ready_k, tailed_k, loose_k, recv_ref, left_ref, m_ref, product_ref, *rest):
    *in_refs, out_ref, held, rows, done, recv, recv_sem, sem = rest
    slots, count = out_ref.shape[:2]
    table = pltpu.make_async_copy(recv_ref, recv, recv_sem)
    table.start()
    for i, k in enumerate(ready_k):
        held[pl.ds(k * CAP, CAP)] = product_ref[pl.ds(i * CAP, CAP)]
    left = left_ref[...]
    for k, ref in zip(tailed_k, in_refs):
        rows[k] = ref[CAP * count :]
        if k not in ready_k:
            for r, value in enumerate(multiply(left, parts_of(ref, count))):
                held[k * CAP + r] = value
    for k, ref in zip(loose_k, in_refs[len(tailed_k) :]):
        rows[k] = ref[...]
    m1, m2 = m_ref[0], m_ref[1]
    group = 4
    table.wait()

    def write(j):
        part = pl.ds(j * group, group)
        return pltpu.make_async_copy(done.at[part], out_ref.at[part], sem.at[j])

    for j in range(slots // group):
        for n in range(j * group, (j + 1) * group):
            index = recv[0, n]
            k, r = split_by(index, CAP)
            p1 = rows[k, pl.ds(r, 1)]
            p2 = rows[k, pl.ds(r + CAP, 1)]
            done[n] = held[index] + m1 * p1 + m2 * p2
        write(j).start()
    for j in range(slots // group):
        write(j).wait()


def call(kernel, out_shape, in_specs, out_specs, args, scratch=(), aliases=None):
    return pl.pallas_call(
        kernel,
        out_shape=out_shape,
        in_specs=in_specs,
        out_specs=out_specs,
        scratch_shapes=scratch,
        input_output_aliases=aliases or {},
        compiler_params=pltpu.CompilerParams(vmem_limit_bytes=GRANT),
    )(*args)


def f32(*shape):
    return jax.ShapeDtypeStruct(shape, jnp.float32)


def i32(*shape):
    return jax.ShapeDtypeStruct(shape, jnp.int32)


def shifts(size):
    return [
        (i, i + 2 if i + 2 < size else i - 1) if i % 2 else (i, i - 2 if i >= 2 else i + 1)
        for i in range(size)
    ]


def swaps(size, odd):
    if not odd:
        return [(i, i ^ 1) for i in range(size)]
    return [(i, min(max(((i + 1) ^ 1) - 1, 0), size - 1)) for i in range(size)]


def distances(slabs):
    chips = slabs // 2
    early = range(chips // 2, chips - max(1, chips // 8))
    return [k for k in range(1, chips) if k not in early], list(early)


def shards(
    pressure, storage, trans, source, shells_old, shell_cap, shell_trans, new_source, cell_block
):
    slabs, cols = lax.axis_size("slab"), lax.axis_size("col")
    height, width = pressure.shape
    old_slots, count, cells = shells_old.shape[1:]
    new_slots = new_source.shape[1] // slabs
    chips = slabs // 2
    shells = shells_old[0]
    cap_row, trans_row = shell_cap.reshape(1, count), shell_trans.reshape(1, count)

    tall = height + 2 * EDGE
    tail = STEPS * CAP
    late_k, early_k = distances(slabs)

    def chip_swap(value, k):
        return lax.ppermute(value, "slab", [(i, i ^ (2 * k)) for i in range(slabs)])

    hopped = lax.ppermute(shells, "slab", swaps(slabs, False))
    plane, edge = f32(height, width), f32(FIELDS, EDGE, width)
    (
        inverse, const, slot, place, recv, cap_row, trans_row, held,
        pressure, storage, trans, source, base1, base2, coef, edge_a, edge_b,
    ) = call(
        base_kernel,
        (
            f32(count, LANES), f32(1, LANES), i32(1, chips * CAP), i32(1, slabs * CAP),
            i32(1, new_slots), f32(1, count), f32(1, count), f32(old_slots, count, cells),
            *(plane,) * 7, edge, edge,
        ),
        [HBM] * 9,
        (VMEM,) * 17,
        tuple(
            pltpu.with_memory_space_constraint(value, pltpu.HBM)
            for value in (
                cap_row, trans_row, new_source, cell_block, shells, pressure, storage, trans, source
            )
        ),
        [
            pltpu.VMEM((3, width // LANES, height, LANES), jnp.float32),
            pltpu.VMEM(new_source.shape, jnp.int32),
            pltpu.VMEM(cell_block.shape, jnp.int32),
            pltpu.SMEM(cell_block.shape, jnp.int32),
            pltpu.SemaphoreType.DMA((9,)),
            pltpu.SemaphoreType.DMA((4,)),
        ],
    )
    edge_b = lax.ppermute(edge_b, "slab", shifts(slabs))
    edge_b = lax.ppermute(edge_b, "slab", swaps(slabs, False))
    edge_a = lax.ppermute(edge_a, "slab", swaps(slabs, False))
    packed = call(
        pack_kernel,
        tuple(f32(CAP * count + (tail if k in late_k else 0), cells) for k in range(chips)),
        [VMEM, VMEM, VMEM],
        (VMEM,) * chips,
        (slot, held, hopped),
    )
    side = call(
        side_kernel,
        f32(tall, LANES),
        [VMEM] * 9,
        VMEM,
        (pressure, storage, trans, source, base1, base2, coef, edge_a, edge_b),
    )
    side_c = lax.ppermute(side, "col", swaps(cols, False))
    side_d = lax.ppermute(side, "col", swaps(cols, True)) if cols > 2 else side_c
    blocks = {0: packed[0]}
    for k in early_k:
        blocks[k] = chip_swap(packed[k], k)

    result, rows = call(
        fracture_kernel,
        (plane, f32(slabs, tail, LANES)),
        [VMEM] * 13,
        (VMEM, VMEM),
        (
            place, const, pressure, storage, trans, source, base1, base2, coef,
            edge_a, edge_b, side_c, side_d,
        ),
        [
            pltpu.VMEM((STEPS, width // LANES, height, LANES), jnp.float32),
            pltpu.SMEM(place.shape, jnp.int32),
            pltpu.SemaphoreType.DMA,
        ],
    )
    other_rows = lax.ppermute(rows, "slab", swaps(slabs, False))
    local_rows, *filled = call(
        functools.partial(rows_kernel, late_k, early_k),
        (f32(tail, cells),)
        + (f32(CAP * count + tail, cells),) * len(late_k)
        + (f32(tail, cells),) * len(early_k),
        [VMEM] * (2 + len(late_k)),
        (VMEM,) * chips,
        (rows, other_rows, *(packed[k] for k in late_k)),
        aliases={2 + i: 1 + i for i in range(len(late_k))},
    )
    for k, value in zip(late_k, filled):
        blocks[k] = chip_swap(value, k)
    loose = [chip_swap(value, k) for k, value in zip(early_k, filled[len(late_k) :])]
    ready_k = [k for k in range(chips) if k not in late_k]
    left, coefficients, product = call(
        product_kernel,
        (
            jax.ShapeDtypeStruct((count, 3 * count), jnp.bfloat16),
            f32(2, count, LANES),
            f32(len(ready_k) * CAP, count, cells),
        ),
        [VMEM] * (3 + len(ready_k)),
        (VMEM,) * 3,
        (cap_row, trans_row, inverse, *(blocks[k] for k in ready_k)),
    )
    loose_k = [0, *early_k]
    shells_new = call(
        functools.partial(final_kernel, ready_k, late_k, loose_k),
        f32(new_slots, count, cells),
        [VMEM] * (4 + chips),
        ANY,
        (
            recv, left, coefficients, product,
            *(blocks[k] for k in late_k), local_rows, *loose,
        ),
        [
            pltpu.VMEM((chips * CAP, count, cells), jnp.float32),
            pltpu.VMEM((chips, tail, cells), jnp.float32),
            pltpu.VMEM((new_slots, count, cells), jnp.float32),
            pltpu.SMEM(recv.shape, jnp.int32),
            pltpu.SemaphoreType.DMA,
            pltpu.SemaphoreType.DMA((new_slots // 4,)),
        ],
    )
    return (result, shells_new[None])


def solution(mesh):
    placed_at = (
        P("slab", "col"),
        P("slab", "col"),
        P("slab", "col"),
        P("slab", "col"),
        P("col", "slab", None, None),
        P(),
        P(),
        P("col", None),
        P("col", "slab"),
    )
    return jax.shard_map(
        shards,
        mesh=mesh,
        in_specs=placed_at,
        out_specs=(P("slab", "col"), P("col", "slab", None, None)),
        check_vma=False,
    )
```
